128 devices in a mesh: tm: 4 (over x), det: 32 (over z, y, core).
Axes of the slice: x: 4, y: 4, z: 4, core: 2. Of those that a mesh axis runs over, the one named last changes fastest.
Arguments:
- timestream: float32 [4, 512, 8192], P('tm', 'det'), may hold values from -0.8 to 0.8
- polar_angle: float32 [4, 512, 8192], P('tm', 'det'), may hold values from -3.140625 to 3.140625
- pixel_index: int32 [4, 512, 8192], P('tm', 'det'), may hold values from 0 to 2047
- strip_tile: int32 [4, 512, 64], P('tm', 'det'), may hold values from 0 to 31
- time_const: float32 [4, 512], P('tm', 'det'), may hold values from 0.2 to 2
- knee_freq: float32 [4, 512], P('tm', 'det'), may hold values from 0.005 to 0.05
- noise_slope: float32 [4, 512], P('tm', 'det'), may hold values from 1 to 3
- white_weight: float32 [4, 512], P('tm', 'det'), may hold values from 0.5 to 2
- mode_mix: float32 [4, 512, 64], P('tm', 'det'), may hold values from -0.5 to 0.5
- coupling: float32 [64, 64], replicated, may hold values from -1 to 2
- device_slots: int32 [4, 1024], P('tm', 'det'), may hold values from 0 to 127, as said below
- slot_home: int32 [4, 128], P('tm', 'det'), may hold values from 0 to 31, as said below
Outputs:
- sky_map: float32 [1024, 3, 2048], P(('tm', 'det'))
The draws below stay inside these ranges and needn't reach their ends.
Inputs may be any that keep to these rules, and one draw needn't show every extreme that they name: `device_slots`: entries j * 32 to (j + 1) * 32 - 1 of a row are the entries of the group's tile list that device j of the group touches, all distinct. Of each block of 4 entries (those with the same entry // 4) a device touches exactly 2 in half of the blocks and exactly 0 in the others. `slot_home`: entry s of group g is owner_tm * 8 + place: the tile is held at place place by the device with tm index owner_tm and det index s // 4. Entries of one block of 4 are distinct; in every block exactly 2 entries share one owner_tm, and the others are spread as evenly as possible over the other owner_tm values.
All inputs are finite; a program needn't handle non-finite values.
Results may differ from the reference program's by a relative error of at most 0.0001.
Values sent between devices are 32-bit elements; how exact they have to be, the bound alone decides.
No kernel may reach another device: no remote copies, remote signals or barrier semaphores. Data moves between devices by JAX's collectives and lax.ppermute only.
A program may use at most 64 MiB of HBM per device.

```python
import math
import jax
import jax.numpy as jnp
from jax import lax

SAMPLES = 4096
SCANS = 2
STRIP = 128
TILE_PIX = 2048
MODES = 64
DET_DEV = 16
GSHARE = 4
TOUCH = 1
CAPD = 2
CAPT = 2
OWN = 8
DETS = 512
STRIPS = 64
GLOCAL = 128
DEV_TILES = 32
N_TM = 4
N_DET = 32


def draw_coupling(key, part):
    first_key, second_key = jax.random.split(jax.random.fold_in(key, 5))
    diagonal = jax.random.uniform(first_key, (MODES,), jnp.float32, 0.5, 1.5)
    spread = 0.3
    offdiag = jax.random.normal(second_key, (MODES, MODES), jnp.float32) * (spread / math.sqrt(MODES))
    offdiag = jnp.clip(offdiag, -0.4, 0.4)
    return offdiag + jnp.diag(diagonal)


def device_pick(device_key):
    order_key, pick_key, shuffle_key = jax.random.split(device_key, 3)
    block_order = jax.random.permutation(order_key, N_DET)
    block_rank = jnp.argsort(block_order)
    pattern = jnp.where(jnp.arange(N_DET) % 2 == 0, CAPD, 2 * TOUCH - CAPD)
    counts = pattern[block_rank]
    block_shuffle = jax.vmap(lambda sub_key: jax.random.permutation(sub_key, GSHARE))(jax.random.split(pick_key, N_DET))
    chosen = block_shuffle[:, :CAPD]
    candidates = jnp.arange(N_DET, dtype=jnp.int32)[:, None] * GSHARE + chosen
    usable = jnp.arange(CAPD)[None, :] < counts[:, None]
    positions = jnp.arange(N_DET * CAPD, dtype=jnp.int32).reshape(N_DET, CAPD)
    sort_keys = jnp.where(usable, positions, positions + N_DET * CAPD).reshape(-1)
    picked = candidates.reshape(-1)[jnp.argsort(sort_keys)[:TOUCH * N_DET]]
    return picked[jax.random.permutation(shuffle_key, TOUCH * N_DET)]


def draw_device_slots(key, part):
    device_keys = jax.random.split(jax.random.fold_in(key, 11), N_TM * N_DET)
    picks = jax.vmap(device_pick)(device_keys)
    return picks.reshape(N_TM, N_DET * TOUCH * N_DET).astype(jnp.int32)


def block_homes(block_key):
    owner_key, place_key, shuffle_key = jax.random.split(block_key, 3)
    owners = jax.random.permutation(owner_key, N_TM)
    ranks_in = jnp.arange(GSHARE, dtype=jnp.int32)
    extra = jnp.maximum(ranks_in - CAPT, 0)
    owner_pos = jnp.where(ranks_in < CAPT, 0, 1 + extra % (N_TM - 1))
    place_rank = jnp.where(ranks_in < CAPT, ranks_in, extra // (N_TM - 1))
    places = jax.vmap(lambda sub_key: jax.random.permutation(sub_key, OWN))(jax.random.split(place_key, N_TM))
    owner_tm = owners[owner_pos]
    home_code = owner_tm * OWN + places[owner_tm, place_rank]
    return home_code[jax.random.permutation(shuffle_key, GSHARE)]


def draw_slot_home(key, part):
    block_keys = jax.random.split(jax.random.fold_in(key, 23), N_TM * N_DET)
    homes = jax.vmap(block_homes)(block_keys)
    return homes.reshape(N_TM, N_DET * GSHARE).astype(jnp.int32)


def plant(values, own_key, low, high):
    dims = values.shape
    place = [jax.random.randint(jax.random.fold_in(own_key, axis), (), 0, dims[axis]) for axis in range(len(dims))]
    values = values.at[tuple(place)].set(low)
    longest = dims.index(max(dims))
    place[longest] = (place[longest] + 1) % dims[longest]
    return values.at[tuple(place)].set(high)


def block_scale(stream_key, shape, cuts, low, largest):
    factor_of = 1.0
    for axis_at, parts in cuts:
        heights = jax.random.uniform(jax.random.fold_in(jax.random.fold_in(stream_key, 6), axis_at), (parts,), jnp.float32, low / len(cuts), largest / len(cuts))
        factor_of = factor_of * jnp.repeat(jnp.exp(heights), shape[axis_at] // parts).reshape((-1,) + (1,) * (len(shape) - 1 - axis_at))
    return factor_of


def noise(key, extent, scale, most, cuts=(), kind=jnp.bfloat16):
    array = jax.random.normal(key, extent, jnp.float32) * scale
    if len(cuts) > 0:
        array = block_scale(key, extent, cuts, -0.22, 0.18) * array
    return jnp.clip(array, min=-most, max=most).astype(kind)


def setup_inputs(seed: int = 0) -> dict:
    arg_keys = jax.random.split(jax.random.key(seed), 13)
    timestream = noise(arg_keys[0], (N_TM, DETS, SCANS * SAMPLES), 0.1, 0.8, ((0, 4), (1, 32)), jnp.float32)
    polar_angle = jnp.clip(jax.random.uniform(arg_keys[1], (N_TM, DETS, SCANS * SAMPLES), jnp.float32, -3.140625, 3.140625), -3.140625, 3.140625)
    pixel_index = plant(jax.random.randint(arg_keys[2], (N_TM, DETS, SCANS * SAMPLES), 0, TILE_PIX), jax.random.fold_in(arg_keys[2], 1), 0, TILE_PIX - 1).astype(jnp.int32)
    strip_tile = plant(jax.random.randint(arg_keys[3], (N_TM, DETS, STRIPS), 0, TOUCH * N_DET), jax.random.fold_in(arg_keys[3], 1), 0, (TOUCH * N_DET) - 1).astype(jnp.int32)
    time_const = jnp.clip(jnp.exp(math.log(2.0) - 2.3025851 * jax.random.uniform(arg_keys[4], (N_TM, DETS), jnp.float32) ** block_scale(arg_keys[4], (N_TM, DETS), ((0, 4), (1, 32)), -0.2, 0.2)), 0.2, 2.0)
    knee_freq = jnp.clip(jnp.exp(math.log(0.05) - 2.3025851 * jax.random.uniform(arg_keys[5], (N_TM, DETS), jnp.float32) ** block_scale(arg_keys[5], (N_TM, DETS), ((0, 4), (1, 32)), -0.2, 0.2)), 0.005, 0.05)
    noise_slope = jnp.clip(1.0 + 2.0 * jax.random.uniform(arg_keys[6], (N_TM, DETS), jnp.float32) ** block_scale(arg_keys[6], (N_TM, DETS), ((0, 4), (1, 32)), -0.2, 0.2), 1.0, 3.0)
    white_weight = jnp.clip(jnp.exp(math.log(2.0) - 1.3862944 * jax.random.uniform(arg_keys[7], (N_TM, DETS), jnp.float32) ** block_scale(arg_keys[7], (N_TM, DETS), ((0, 4), (1, 32)), -0.2, 0.2)), 0.5, 2.0)
    mode_mix = noise(arg_keys[8], (N_TM, DETS, MODES), (DETS // 4) ** -0.5, 0.5, ((0, 4), (1, 32)), jnp.float32)
    coupling = draw_coupling(jax.random.fold_in(arg_keys[12], 71), 0)
    device_slots = draw_device_slots(jax.random.fold_in(arg_keys[12], 71), 0)
    slot_home = draw_slot_home(jax.random.fold_in(arg_keys[12], 71), 0)
    return {"timestream": timestream, "polar_angle": polar_angle, "pixel_index": pixel_index, "strip_tile": strip_tile, "time_const": time_const, "knee_freq": knee_freq, "noise_slope": noise_slope, "white_weight": white_weight, "mode_mix": mode_mix, "coupling": coupling, "device_slots": device_slots, "slot_home": slot_home}


HIGHEST = lax.Precision.HIGHEST


def frequency_axis():
    positions = jnp.arange(SAMPLES, dtype=jnp.int32)
    return ((positions + SAMPLES // 2) % SAMPLES - SAMPLES // 2).astype(jnp.float32) / SAMPLES


def filtered(stream, time_const, knee_freq, noise_slope, white_weight, mode_mix, coupling):
    spectrum = jnp.fft.fft(stream, axis=-1)
    real_part = jnp.real(spectrum)
    imag_part = jnp.imag(spectrum)
    frequency = frequency_axis()
    power_law = jnp.power(jnp.abs(frequency)[None, :], noise_slope[:, None])
    weight = white_weight[:, None] * power_law / (power_law + jnp.power(knee_freq[:, None], noise_slope[:, None]))
    lag_phase = 2.0 * math.pi * frequency[None, :] * time_const[:, None]
    weighted_real = weight * (real_part - lag_phase * imag_part)
    weighted_imag = weight * (imag_part + lag_phase * real_part)
    stacked = jnp.concatenate([weighted_real, weighted_imag], axis=1)
    amplitudes = jnp.dot(mode_mix.T, stacked, precision=HIGHEST, preferred_element_type=jnp.float32)
    coupled = jnp.dot(coupling, amplitudes, precision=HIGHEST, preferred_element_type=jnp.float32)
    projected = jnp.dot(mode_mix, coupled, precision=HIGHEST, preferred_element_type=jnp.float32)
    weight_pair = jnp.concatenate([weight, weight], axis=1)
    cleaned = stacked - weight_pair * projected
    complexed = cleaned[:, :SAMPLES] + 1j * cleaned[:, SAMPLES:]
    return jnp.real(jnp.fft.ifft(complexed, axis=-1))


def group_partials(stream, polar_angle, pixel_index, strip_tile, slot_list):
    slot_table = slot_list.reshape(N_DET, DEV_TILES)
    owner_device = jnp.arange(DETS, dtype=jnp.int32) // DET_DEV
    strip_group = slot_table[owner_device[:, None], strip_tile]
    sample_slot = jnp.repeat(strip_group, STRIP, axis=1)
    flat_index = (sample_slot * (3 * TILE_PIX) + pixel_index).reshape(-1)
    values = stream.reshape(-1)
    twice = 2.0 * polar_angle.reshape(-1)
    segment_ids = jnp.concatenate([flat_index, flat_index + TILE_PIX, flat_index + 2 * TILE_PIX])
    payload = jnp.concatenate([values, values * jnp.cos(twice), values * jnp.sin(twice)])
    sums = jax.ops.segment_sum(payload, segment_ids, num_segments=GLOCAL * 3 * TILE_PIX)
    return sums.reshape(GLOCAL, 3, TILE_PIX)


def reference(timestream, polar_angle, pixel_index, strip_tile, time_const, knee_freq, noise_slope, white_weight, mode_mix, coupling, device_slots, slot_home):
    sky_map = jnp.zeros((N_TM * N_DET * OWN, 3, TILE_PIX), jnp.float32)
    slot_counter = jnp.arange(GLOCAL, dtype=jnp.int32)
    for group_index in range(N_TM):
        pieces = []
        for scan_index in range(SCANS):
            segment = timestream[group_index, :, scan_index * SAMPLES:(scan_index + 1) * SAMPLES]
            pieces.append(filtered(segment, time_const[group_index], knee_freq[group_index], noise_slope[group_index], white_weight[group_index], mode_mix[group_index], coupling))
        cleaned = jnp.concatenate(pieces, axis=1)
        partials = group_partials(cleaned, polar_angle[group_index], pixel_index[group_index], strip_tile[group_index], device_slots[group_index])
        home_code = slot_home[group_index]
        target_rows = ((home_code // OWN) * N_DET + slot_counter // GSHARE) * OWN + home_code % OWN
        sky_map = sky_map + jax.ops.segment_sum(partials, target_rows, num_segments=N_TM * N_DET * OWN)
    return sky_map
```

```python
import math

import jax
import jax.numpy as jnp
import numpy as np
from jax import lax
from jax.experimental import pallas as pl
from jax.experimental.pallas import tpu as pltpu
from jax.sharding import PartitionSpec as P

SAMPLES = 4096
OUTER = 32
INNER = 128
DETS = 16
PEERS = 32
STRIPS = 64
MODES = 64
TM = 4
OWN = 8
ROWS = 48

HIGHEST = lax.Precision.HIGHEST
VMEM = pltpu.VMEM
SMEM = pltpu.SMEM


def tables():
    outer = np.arange(OUTER)[:, None]
    inner = np.arange(INNER)[None, :]
    twist = 2.0 * math.pi * outer * inner / SAMPLES
    grid = 2.0 * math.pi * np.outer(np.arange(INNER), np.arange(INNER)) / INNER
    cos_in, sin_in = np.cos(grid), np.sin(grid)
    forward = np.block([[cos_in, -sin_in], [sin_in, cos_in]])
    inverse = np.block([[cos_in, sin_in], [-sin_in, cos_in]]) / SAMPLES
    index = outer + OUTER * inner
    signed = (index + SAMPLES // 2) % SAMPLES - SAMPLES // 2
    freq = signed / SAMPLES
    log_freq = np.where(signed == 0, -1e30, np.log(np.maximum(np.abs(freq), 1e-9)))
    lag = np.where(signed == -(SAMPLES // 2), 0.0, 2.0 * math.pi * freq)
    return [
        np.asarray(t, np.float32)
        for t in (np.cos(twist), np.sin(twist), forward, inverse, log_freq, lag)
    ]


def transform(points, sign):
    count = len(points)
    if count == 1:
        return points
    even = transform(points[0::2], sign)
    odd = transform(points[1::2], sign)
    first, second = [], []
    half = count // 2
    for k in range(half):
        re, im = odd[k]
        angle = sign * 2.0 * math.pi * k / count
        c, s = math.cos(angle), math.sin(angle)
        if k == 0:
            tr, ti = re, im
        elif 4 * k == count:
            tr, ti = (-im, re) if sign > 0 else (im, -re)
        else:
            tr, ti = c * re - s * im, c * im + s * re
        er, ei = even[k]
        first.append((er + tr, ei + ti))
        second.append((er - tr, ei - ti))
    return first + second


def column(row):
    rows = lax.broadcasted_iota(jnp.int32, (DETS, DETS), 0)
    cols = lax.broadcasted_iota(jnp.int32, (DETS, DETS), 1)
    return jnp.sum(jnp.where(rows == cols, row, 0.0), axis=1, keepdims=True)


def forward_kernel(
    slots, signal, tau, knee, slope, white, mix, cos_t, sin_t, matrix, log_f, lag_f,
    out, weight_out, scratch,
):
    for half in range(2):
        lo = 8 * half
        points = [
            (
                signal[lo : lo + 8, a * INNER : (a + 1) * INNER],
                signal[lo : lo + 8, (OUTER + a) * INNER : (OUTER + a + 1) * INNER],
            )
            for a in range(OUTER)
        ]
        for k, (re, im) in enumerate(transform(points, -1)):
            c = cos_t[k : k + 1, :]
            s = sin_t[k : k + 1, :]
            scratch[k * DETS + lo : k * DETS + lo + 8, 0:INNER] = re * c + im * s
            scratch[k * DETS + lo : k * DETS + lo + 8, INNER : 2 * INNER] = im * c - re * s
    tau_c = jnp.broadcast_to(column(tau[...]), (DETS, INNER))
    slope_c = jnp.broadcast_to(column(slope[...]), (DETS, INNER))
    white_c = jnp.broadcast_to(column(white[...]), (DETS, INNER))
    knee_c = jnp.broadcast_to(column(knee[...]), (DETS, INNER))
    knee_p = jnp.exp(slope_c * jnp.log(knee_c))
    group = 8
    for start in range(0, OUTER, group):
        spec = jnp.dot(
            scratch[start * DETS : (start + group) * DETS, :],
            matrix[...],
            precision=HIGHEST,
            preferred_element_type=jnp.float32,
        )
        for step in range(group):
            k = start + step
            power = jnp.exp(slope_c * log_f[k : k + 1, :])
            weight = white_c * power / (power + knee_p)
            lag = tau_c * lag_f[k : k + 1, :]
            re = spec[step * DETS : (step + 1) * DETS, 0:INNER]
            im = spec[step * DETS : (step + 1) * DETS, INNER : 2 * INNER]
            weight_out[k] = weight
            out[k, 0:DETS, :] = weight * (re - lag * im)
            out[k, DETS : 2 * DETS, :] = weight * (im + lag * re)
    mixed = jnp.concatenate([mix[0:8, :], mix[8:16, :]], axis=1)
    for k in range(OUTER):
        out[k, 32:40, :] = mixed
        out[k, 40:48, :] = jnp.full((8, INNER), -1.0, jnp.float32)

    def mark(entry, carry):
        slot = slots[0, entry]
        block = slot // 4

        def earlier(other, rank):
            return rank + jnp.where(slots[0, other] // 4 == block, 1, 0)

        rank = lax.fori_loop(0, entry, earlier, 0)
        rows = lax.broadcasted_iota(jnp.int32, (8, INNER), 0)
        value = (slot - 4 * block).astype(jnp.float32)
        old = out[block, 40:48, :]
        out[block, 40:48, :] = jnp.where(rows == rank, value, old)
        return carry

    lax.fori_loop(0, PEERS, mark, 0)


def couple_kernel(got, coupling, out, labels):
    amps = None
    mixes = []
    for half in range(2):
        lo = 8 * half
        re = got[:, lo : lo + 8, :].reshape(PEERS * 8, INNER)
        im = got[:, DETS + lo : DETS + lo + 8, :].reshape(PEERS * 8, INNER)
        mix = got[:, 32:40, half * MODES : (half + 1) * MODES].reshape(PEERS * 8, MODES)
        both = jnp.concatenate([re, im], axis=1)
        part = lax.dot_general(
            mix, both, (((0,), (0,)), ((), ())),
            precision=HIGHEST, preferred_element_type=jnp.float32,
        )
        amps = part if amps is None else amps + part
        mixes.append(mix)
    coupled = jnp.dot(
        coupling[...], amps, precision=HIGHEST, preferred_element_type=jnp.float32
    )
    for half in range(2):
        lo = 8 * half
        back = jnp.dot(
            mixes[half], coupled, precision=HIGHEST, preferred_element_type=jnp.float32
        )
        out[:, lo : lo + 8, :] = back[:, 0:INNER].reshape(PEERS, 8, INNER)
        out[:, DETS + lo : DETS + lo + 8, :] = back[:, INNER:].reshape(PEERS, 8, INNER)
    labels[...] = got[:, 40:48, :]


def bin_kernel(
    slots, tiles, weighted, weight, back, cosine, sine, pixel, cos_t, sin_t, matrix,
    out, scratch, stream, send_slot,
):
    for k in range(OUTER):
        re = weighted[k, 0:DETS, :] - weight[k] * back[k, 0:DETS, :]
        im = weighted[k, DETS : 2 * DETS, :] - weight[k] * back[k, DETS : 2 * DETS, :]
        scratch[k * DETS : (k + 1) * DETS, 0:INNER] = re
        scratch[k * DETS : (k + 1) * DETS, INNER : 2 * INNER] = im
    group = 8
    for start in range(0, OUTER, group):
        section = jnp.dot(
            scratch[start * DETS : (start + group) * DETS, :],
            matrix[...],
            precision=HIGHEST,
            preferred_element_type=jnp.float32,
        )
        for step in range(group):
            k = start + step
            c = cos_t[k : k + 1, :]
            s = sin_t[k : k + 1, :]
            re = section[step * DETS : (step + 1) * DETS, 0:INNER]
            im = section[step * DETS : (step + 1) * DETS, INNER : 2 * INNER]
            scratch[k * DETS : (k + 1) * DETS, 0:INNER] = re * c - im * s
            scratch[k * DETS : (k + 1) * DETS, INNER : 2 * INNER] = im * c + re * s
    for half in range(2):
        lo = 8 * half
        points = [
            (
                scratch[k * DETS + lo : k * DETS + lo + 8, 0:INNER],
                scratch[k * DETS + lo : k * DETS + lo + 8, INNER : 2 * INNER],
            )
            for k in range(OUTER)
        ]
        for a, (re, im) in enumerate(transform(points, 1)):
            stream[a, lo : lo + 8, :] = re
            stream[OUTER + a, lo : lo + 8, :] = im

    def assign(entry, carry):
        block = slots[0, entry] // 4

        def earlier(other, rank):
            return rank + jnp.where(slots[0, other] // 4 == block, 1, 0)

        send_slot[entry] = 2 * block + lax.fori_loop(0, entry, earlier, 0)
        return carry

    lax.fori_loop(0, PEERS, assign, 0)

    def clear(entry, carry):
        out[entry] = jnp.zeros((ROWS, INNER), jnp.float32)
        return carry

    lax.fori_loop(0, 2 * PEERS, clear, 0)
    lanes = lax.broadcasted_iota(jnp.int32, (16, INNER), 0).astype(jnp.float32)
    marks = [(lanes + 16.0 * g).astype(jnp.bfloat16) for g in range(8)]
    one = jnp.ones((16, INNER), jnp.bfloat16)
    zero = jnp.zeros((16, INNER), jnp.bfloat16)

    def strip(s, carry):
        base = pl.multiple_of(s * INNER, INNER)
        pix = pixel[:, pl.ds(base, INNER)]
        high = (pix >> 7).astype(jnp.float32)
        low = (pix & 127).astype(jnp.float32)
        values = stream[s]
        maps = [values, values * cosine[:, pl.ds(base, INNER)], values * sine[:, pl.ds(base, INNER)]]
        tops = [m.astype(jnp.bfloat16).astype(jnp.float32) for m in maps]
        rests = [m - t for m, t in zip(maps, tops)]
        parts = tops + rests

        def spread(block, d):
            return jnp.broadcast_to(block[d : d + 1, :], (16, INNER)).astype(jnp.bfloat16)

        for d in range(DETS):
            high_d = spread(high, d)
            low_d = spread(low, d)
            hit = high_d == marks[0]
            left = jnp.concatenate(
                [jnp.where(hit, spread(p, d), zero) for p in parts], axis=0
            )
            right = jnp.concatenate(
                [jnp.where(low_d == marks[g], one, zero) for g in range(8)], axis=0
            )
            sums = lax.dot_general(
                left, right, (((1,), (1,)), ((), ())), preferred_element_type=jnp.float32
            )
            slot = send_slot[tiles[d, s]]
            out[slot] = out[slot] + (sums[0:ROWS, :] + sums[ROWS:, :])
        return carry

    lax.fori_loop(0, STRIPS, strip, 0)


def gather_kernel(homes, got, labels, out):
    for place in range(2 * TM):
        out[place, 0:ROWS, :] = jnp.zeros((ROWS, INNER), jnp.float32)
        out[place, ROWS:, :] = jnp.full((8, INNER), -1.0, jnp.float32)
    for tile in range(4):
        def add(source, total):
            for rank in range(2):
                hit = labels[source, rank : rank + 1, :] == float(tile)
                total = total + jnp.where(
                    hit, got[source, rank * ROWS : (rank + 1) * ROWS, :], 0.0
                )
            return total

        total = lax.fori_loop(
            0, PEERS, add, jnp.zeros((ROWS, INNER), jnp.float32), unroll=4
        )
        owner = homes[0, tile] // OWN
        rank = 0
        for other in range(tile):
            rank = rank + jnp.where(homes[0, other] // OWN == owner, 1, 0)
        row = 2 * owner + rank
        out[row, 0:ROWS, :] = total
        place = (homes[0, tile] - OWN * owner).astype(jnp.float32)
        out[row, ROWS:, :] = jnp.broadcast_to(place, (8, INNER))


def place_kernel(got, out):
    for place in range(OWN):
        total = jnp.zeros((ROWS, INNER), jnp.float32)
        for source in range(2 * TM):
            hit = got[source, ROWS : ROWS + 1, :] == float(place)
            total = total + jnp.where(hit, got[source, 0:ROWS, :], 0.0)
        out[place] = total


def call(kernel, outs, specs, *operands, scratch=()):
    return pl.pallas_call(
        kernel,
        out_shape=outs,
        in_specs=[pl.BlockSpec(memory_space=s) for s in specs],
        scratch_shapes=list(scratch),
        compiler_params=pltpu.CompilerParams(vmem_limit_bytes=48 << 20),
    )(*operands)


def per_device(
    timestream, polar_angle, pixel_index, strip_tile, time_const, knee_freq, noise_slope,
    white_weight, mode_mix, coupling, device_slots, slot_home,
):
    f32 = jnp.float32
    cos_t, sin_t, forward, inverse, log_f, lag_f = [jnp.asarray(t) for t in tables()]
    packed, weight = call(
        forward_kernel,
        (
            jax.ShapeDtypeStruct((PEERS, 48, INNER), f32),
            jax.ShapeDtypeStruct((PEERS, DETS, INNER), f32),
        ),
        [SMEM] + [VMEM] * 11,
        device_slots, timestream[0], time_const, knee_freq, noise_slope, white_weight,
        mode_mix[0], cos_t, sin_t, forward, log_f, lag_f,
        scratch=[VMEM((OUTER * DETS, 2 * INNER), f32)],
    )
    got = lax.all_to_all(packed, "det", 0, 0, tiled=True)
    projected, labels = call(
        couple_kernel,
        (
            jax.ShapeDtypeStruct((PEERS, 2 * DETS, INNER), f32),
            jax.ShapeDtypeStruct((PEERS, 8, INNER), f32),
        ),
        [VMEM] * 2,
        got, coupling,
    )
    back = lax.all_to_all(projected, "det", 0, 0, tiled=True)
    twice = 2.0 * polar_angle[0]
    partials = call(
        bin_kernel,
        jax.ShapeDtypeStruct((2 * PEERS, ROWS, INNER), f32),
        [SMEM] * 2 + [VMEM] * 9,
        device_slots, strip_tile[0], packed, weight, back, jnp.cos(twice), jnp.sin(twice),
        pixel_index[0], cos_t, sin_t, inverse,
        scratch=[
            VMEM((OUTER * DETS, 2 * INNER), f32),
            VMEM((STRIPS, DETS, INNER), f32),
            SMEM((PEERS,), jnp.int32),
        ],
    )
    parts = lax.all_to_all(
        partials.reshape(PEERS, 2 * ROWS, INNER), "det", 0, 0, tiled=True
    )
    owned = call(
        gather_kernel,
        jax.ShapeDtypeStruct((2 * TM, ROWS + 8, INNER), f32),
        [SMEM] + [VMEM] * 2,
        slot_home, parts, labels,
    )
    final = lax.all_to_all(
        owned.reshape(TM, 2 * (ROWS + 8), INNER), "tm", 0, 0, tiled=True
    )
    placed = call(
        place_kernel,
        jax.ShapeDtypeStruct((OWN, ROWS, INNER), f32),
        [VMEM],
        final.reshape(2 * TM, ROWS + 8, INNER),
    )
    return placed.reshape(OWN, 3, 16 * INNER)


def solution(mesh):
    strips = P("tm", "det", None)
    dets = P("tm", "det")
    return jax.shard_map(
        per_device,
        mesh=mesh,
        in_specs=(strips,) * 4 + (dets,) * 4 + (strips, P(), dets, dets),
        out_specs=P(("tm", "det"), None, None),
        check_vma=False,
    )
```

```python
import math

import jax
import jax.numpy as jnp
import numpy as np
from jax import lax
from jax.experimental import pallas as pl
from jax.experimental.pallas import tpu as pltpu
from jax.sharding import PartitionSpec as P

SAMPLES = 4096
OUTER = 32
INNER = 128
DETS = 16
PEERS = 32
STRIPS = 64
MODES = 64
TM = 4
OWN = 8
UNROLL = 4
ROWS = 48

HIGHEST = lax.Precision.HIGHEST
VMEM = pltpu.VMEM
SMEM = pltpu.SMEM
HBM = pltpu.HBM


def tables():
    outer = np.arange(OUTER)[:, None]
    inner = np.arange(INNER)[None, :]
    twist = 2.0 * math.pi * outer * inner / SAMPLES
    grid = 2.0 * math.pi * np.outer(np.arange(INNER), np.arange(INNER)) / INNER
    cos_in, sin_in = np.cos(grid), np.sin(grid)
    forward = np.block([[cos_in, -sin_in], [sin_in, cos_in]])
    inverse = np.block([[cos_in, sin_in], [-sin_in, cos_in]]) / SAMPLES
    index = outer + OUTER * inner
    signed = (index + SAMPLES // 2) % SAMPLES - SAMPLES // 2
    freq = signed / SAMPLES
    log_freq = np.where(signed == 0, -1e30, np.log(np.maximum(np.abs(freq), 1e-9)))
    lag = np.where(signed == -(SAMPLES // 2), 0.0, 2.0 * math.pi * freq)
    rows = np.concatenate([np.cos(twist), np.sin(twist), log_freq, lag], axis=0)
    rows, forward, inverse = [np.asarray(t, np.float32) for t in (rows, forward, inverse)]
    top = inverse.astype(jnp.bfloat16)
    rest = (inverse - top.astype(np.float32)).astype(jnp.bfloat16)
    return rows, forward, np.stack([top, rest])


def transform(points, sign):
    count = len(points)
    if count == 1:
        return points
    even = transform(points[0::2], sign)
    odd = transform(points[1::2], sign)
    first, second = [], []
    half = count // 2
    for k in range(half):
        re, im = odd[k]
        angle = sign * 2.0 * math.pi * k / count
        c, s = math.cos(angle), math.sin(angle)
        if k == 0:
            tr, ti = re, im
        elif 4 * k == count:
            tr, ti = (-im, re) if sign > 0 else (im, -re)
        else:
            tr, ti = c * re - s * im, c * im + s * re
        er, ei = even[k]
        first.append((er + tr, ei + ti))
        second.append((er - tr, ei - ti))
    return first + second


def split(x):
    top = x.astype(jnp.bfloat16)
    return top, (x - top.astype(jnp.float32)).astype(jnp.bfloat16)


def product(left, right, dims=(((1,), (0,)), ((), ()))):
    def dot(a, b):
        return lax.dot_general(a, b, dims, preferred_element_type=jnp.float32)

    return dot(left[0], right[0]) + (dot(left[0], right[1]) + dot(left[1], right[0]))


def column(row):
    rows = lax.broadcasted_iota(jnp.int32, (DETS, DETS), 0)
    cols = lax.broadcasted_iota(jnp.int32, (DETS, DETS), 1)
    return jnp.sum(jnp.where(rows == cols, row, 0.0), axis=1, keepdims=True)


def ranks(slots, counts, mark):
    for block in range(PEERS):
        counts[block] = 0
    for entry in range(PEERS):
        slot = slots[0, entry]
        block = slot >> 2
        rank = counts[block]
        counts[block] = rank + 1
        mark(entry, slot, block, rank)


def forward_kernel(
    slots_h, signal_h, tau_h, knee_h, slope_h, white_h, mix_h, rows_h, matrix_h,
    out, weight_out, scratch, slots, signal, tau, knee, slope, white, mix, rows, matrix,
    counts, sems,
):
    pairs = [
        (signal_h.at[0], signal), (rows_h, rows), (slots_h, slots), (tau_h, tau),
        (knee_h, knee), (slope_h, slope), (white_h, white), (mix_h.at[0], mix),
        (matrix_h, matrix),
    ]
    copies = [pltpu.make_async_copy(a, b, sems.at[i]) for i, (a, b) in enumerate(pairs)]
    for copy in copies:
        copy.start()
    for copy in copies[2:8]:
        copy.wait()
    mixed = jnp.concatenate([mix[0:8, :], mix[8:16, :]], axis=1)
    for k in range(OUTER):
        out[k, 32:40, :] = mixed
        out[k, 40:48, :] = jnp.full((8, INNER), -1.0, jnp.float32)

    def mark(entry, slot, block, rank):
        value = (slot - 4 * block).astype(jnp.float32)
        out[block, pl.ds(40 + rank, 1), :] = jnp.broadcast_to(value, (1, INNER))

    ranks(slots, counts, mark)
    for copy in copies[0:2]:
        copy.wait()
    for half in range(2):
        lo = 8 * half
        points = [
            (
                signal[lo : lo + 8, a * INNER : (a + 1) * INNER],
                signal[lo : lo + 8, (OUTER + a) * INNER : (OUTER + a + 1) * INNER],
            )
            for a in range(OUTER)
        ]
        for k, (re, im) in enumerate(transform(points, -1)):
            c = rows[k : k + 1, :]
            s = rows[OUTER + k : OUTER + k + 1, :]
            scratch[k * DETS + lo : k * DETS + lo + 8, 0:INNER] = re * c + im * s
            scratch[k * DETS + lo : k * DETS + lo + 8, INNER : 2 * INNER] = im * c - re * s
    tau_c = jnp.broadcast_to(column(tau[...]), (DETS, INNER))
    slope_c = jnp.broadcast_to(column(slope[...]), (DETS, INNER))
    white_c = jnp.broadcast_to(column(white[...]), (DETS, INNER))
    knee_c = jnp.broadcast_to(column(knee[...]), (DETS, INNER))
    knee_p = jnp.exp(slope_c * jnp.log(knee_c))
    copies[8].wait()
    group = 8
    for start in range(0, OUTER, group):
        spec = jnp.dot(
            scratch[start * DETS : (start + group) * DETS, :],
            matrix[...],
            precision=HIGHEST,
            preferred_element_type=jnp.float32,
        )
        for step in range(group):
            k = start + step
            power = jnp.exp(slope_c * rows[2 * OUTER + k : 2 * OUTER + k + 1, :])
            weight = white_c * power / (power + knee_p)
            lag = tau_c * rows[3 * OUTER + k : 3 * OUTER + k + 1, :]
            re = spec[step * DETS : (step + 1) * DETS, 0:INNER]
            im = spec[step * DETS : (step + 1) * DETS, INNER : 2 * INNER]
            weight_out[k] = weight
            out[k, 0:DETS, :] = weight * (re - lag * im)
            out[k, DETS : 2 * DETS, :] = weight * (im + lag * re)


def couple_kernel(got, coupling_h, out, labels, coupling, sem):
    copy = pltpu.make_async_copy(coupling_h, coupling, sem)
    copy.start()
    amps = None
    mixes = []
    for half in range(2):
        lo = 8 * half
        re = got[:, lo : lo + 8, :].reshape(PEERS * 8, INNER)
        im = got[:, DETS + lo : DETS + lo + 8, :].reshape(PEERS * 8, INNER)
        mix = split(
            got[:, 32:40, half * MODES : (half + 1) * MODES].reshape(PEERS * 8, MODES)
        )
        both = split(jnp.concatenate([re, im], axis=1))
        part = product(mix, both, (((0,), (0,)), ((), ())))
        amps = part if amps is None else amps + part
        mixes.append(mix)
    copy.wait()
    coupled = split(product(split(coupling[...]), split(amps)))
    for half in range(2):
        lo = 8 * half
        back = product(mixes[half], coupled)
        out[:, lo : lo + 8, :] = back[:, 0:INNER].reshape(PEERS, 8, INNER)
        out[:, DETS + lo : DETS + lo + 8, :] = back[:, INNER:].reshape(PEERS, 8, INNER)
    labels[...] = got[:, 40:48, :]


def bin_kernel(
    slots_h, tiles_h, weighted, weight, back, cosine, sine, pixel_h, rows_h, matrix_h,
    out, scratch, stream, slots, tiles, pixel, rows, matrix, counts, parts,
    even, odd, sems,
):
    pairs = [
        (matrix_h, matrix), (rows_h, rows), (slots_h, slots), (tiles_h.at[0], tiles),
        (pixel_h.at[0], pixel),
    ]
    copies = [pltpu.make_async_copy(a, b, sems.at[i]) for i, (a, b) in enumerate(pairs)]
    for copy in copies:
        copy.start()
    for k in range(OUTER):
        re = weighted[k, 0:DETS, :] - weight[k] * back[k, 0:DETS, :]
        im = weighted[k, DETS : 2 * DETS, :] - weight[k] * back[k, DETS : 2 * DETS, :]
        scratch[k * DETS : (k + 1) * DETS, 0:INNER] = re
        scratch[k * DETS : (k + 1) * DETS, INNER : 2 * INNER] = im
    for copy in copies[0:2]:
        copy.wait()
    group = 8
    for start in range(0, OUTER, group):
        section = product(
            split(scratch[start * DETS : (start + group) * DETS, :]), (matrix[0], matrix[1])
        )
        for step in range(group):
            k = start + step
            c = rows[k : k + 1, :]
            s = rows[OUTER + k : OUTER + k + 1, :]
            re = section[step * DETS : (step + 1) * DETS, 0:INNER]
            im = section[step * DETS : (step + 1) * DETS, INNER : 2 * INNER]
            scratch[k * DETS : (k + 1) * DETS, 0:INNER] = re * c - im * s
            scratch[k * DETS : (k + 1) * DETS, INNER : 2 * INNER] = im * c + re * s
    for half in range(2):
        lo = 8 * half
        points = [
            (
                scratch[k * DETS + lo : k * DETS + lo + 8, 0:INNER],
                scratch[k * DETS + lo : k * DETS + lo + 8, INNER : 2 * INNER],
            )
            for k in range(OUTER)
        ]
        for a, (re, im) in enumerate(transform(points, 1)):
            stream[a, lo : lo + 8, :] = re
            stream[OUTER + a, lo : lo + 8, :] = im

    def clear(entry, carry):
        blank = jnp.zeros((ROWS, INNER), jnp.float32)
        even[entry] = jnp.zeros((2 * ROWS, INNER // 2), jnp.float32)
        odd[entry] = jnp.zeros((2 * ROWS, INNER // 2), jnp.float32)
        out[entry] = blank
        out[PEERS + entry] = blank
        return carry

    lax.fori_loop(0, PEERS, clear, 0)
    for copy in copies[2:]:
        copy.wait()
    levels = lax.broadcasted_iota(jnp.int32, (16, INNER), 0).astype(jnp.float32)
    marks = [(levels + 16.0 * g).astype(jnp.bfloat16) for g in range(8)]
    one = jnp.ones((16, INNER), jnp.bfloat16)
    zero = jnp.zeros((16, INNER), jnp.bfloat16)

    def block(start, carry):
        for step in range(UNROLL):
            s = start * UNROLL + step
            base = pl.multiple_of(s * INNER, INNER)
            pix = pixel[:, pl.ds(base, INNER)]
            values = stream[s]
            maps = [
                values,
                values * cosine[:, pl.ds(base, INNER)],
                values * sine[:, pl.ds(base, INNER)],
            ]
            tops = [m.astype(jnp.bfloat16).astype(jnp.float32) for m in maps]
            rests = [m - t for m, t in zip(maps, tops)]
            fields = [
                ((pix >> 7) + 16 * ((pix >> 6) & 1)).astype(jnp.float32),
                (pix & 63).astype(jnp.float32),
            ]
            for i, field in enumerate(fields + tops + rests):
                at = (step * 8 + i) * DETS
                parts[at : at + DETS, :] = field
        for step in range(UNROLL):
            s = start * UNROLL + step

            def spread(i, d):
                row = (step * 8 + i) * DETS + d
                wide = parts[pl.ds(row, 8, stride=0), :]
                return jnp.concatenate([wide, wide], axis=0).astype(jnp.bfloat16)

            for d in range(DETS):
                low_d = spread(1, d)
                high_d = spread(0, d)
                hits = [high_d == marks[0], high_d == marks[1]]
                left = []
                for c in range(6):
                    value = spread(2 + c, d)
                    left += [jnp.where(hit, value, zero) for hit in hits]
                left = jnp.concatenate(left, axis=0)
                right = jnp.concatenate(
                    [jnp.where(low_d == marks[g], one, zero) for g in range(4)], axis=0
                )
                sums = lax.dot_general(
                    left, right, (((1,), (1,)), ((), ())), preferred_element_type=jnp.float32
                )
                tile = tiles[d, s]
                total = (even, odd)[d % 2]
                total[tile] = total[tile] + (sums[0 : 2 * ROWS, :] + sums[2 * ROWS :, :])
        return carry

    lax.fori_loop(0, STRIPS // UNROLL, block, 0)

    def settle(entry, slot, home, rank):
        both = even[entry] + odd[entry]
        for c in range(3):
            out[2 * home + rank, 16 * c : 16 * c + 16, :] = jnp.concatenate(
                [both[32 * c : 32 * c + 16, :], both[32 * c + 16 : 32 * c + 32, :]], axis=1
            )

    ranks(slots, counts, settle)


def gather_kernel(homes, got, labels, out):
    for place in range(2 * TM):
        out[place, 0:ROWS, :] = jnp.zeros((ROWS, INNER), jnp.float32)
        out[place, ROWS:, :] = jnp.full((8, INNER), -1.0, jnp.float32)
    for tile in range(4):
        def add(source, total):
            for rank in range(2):
                hit = labels[source, rank : rank + 1, :] == float(tile)
                total = total + jnp.where(
                    hit, got[source, rank * ROWS : (rank + 1) * ROWS, :], 0.0
                )
            return total

        total = lax.fori_loop(
            0, PEERS, add, jnp.zeros((ROWS, INNER), jnp.float32), unroll=4
        )
        owner = homes[0, tile] // OWN
        rank = 0
        for other in range(tile):
            rank = rank + jnp.where(homes[0, other] // OWN == owner, 1, 0)
        row = 2 * owner + rank
        out[row, 0:ROWS, :] = total
        place = (homes[0, tile] - OWN * owner).astype(jnp.float32)
        out[row, ROWS:, :] = jnp.broadcast_to(place, (8, INNER))


def place_kernel(got, out, totals):
    for place in range(OWN):
        total = jnp.zeros((ROWS, INNER), jnp.float32)
        for source in range(2 * TM):
            hit = got[source, ROWS : ROWS + 1, :] == float(place)
            total = total + jnp.where(hit, got[source, 0:ROWS, :], 0.0)
        totals[place * ROWS : (place + 1) * ROWS, :] = total
    for row in range(ROWS):
        at = (row % 16) * INNER
        out[row // 16, :, at : at + INNER] = totals[pl.ds(row, OWN, stride=ROWS), :]


def call(kernel, outs, specs, *operands, scratch=()):
    operands = [
        pltpu.with_memory_space_constraint(o, HBM) if m is HBM else o
        for o, m in zip(operands, specs)
    ]
    return pl.pallas_call(
        kernel,
        out_shape=outs,
        in_specs=[pl.BlockSpec(memory_space=s) for s in specs],
        scratch_shapes=list(scratch),
        compiler_params=pltpu.CompilerParams(vmem_limit_bytes=48 << 20),
    )(*operands)


def per_device(
    timestream, polar_angle, pixel_index, strip_tile, time_const, knee_freq, noise_slope,
    white_weight, mode_mix, coupling, device_slots, slot_home,
):
    f32 = jnp.float32
    rows, forward, inverse = [jnp.asarray(t) for t in tables()]
    packed, weight = call(
        forward_kernel,
        (
            jax.ShapeDtypeStruct((PEERS, 48, INNER), f32),
            jax.ShapeDtypeStruct((PEERS, DETS, INNER), f32),
        ),
        [HBM] * 9,
        device_slots, timestream, time_const, knee_freq, noise_slope, white_weight,
        mode_mix, rows, forward,
        scratch=[
            VMEM((OUTER * DETS, 2 * INNER), f32),
            SMEM((1, PEERS), jnp.int32),
            VMEM((DETS, 2 * SAMPLES), f32),
            VMEM((1, DETS), f32),
            VMEM((1, DETS), f32),
            VMEM((1, DETS), f32),
            VMEM((1, DETS), f32),
            VMEM((DETS, MODES), f32),
            VMEM((4 * OUTER, INNER), f32),
            VMEM((2 * INNER, 2 * INNER), f32),
            SMEM((PEERS,), jnp.int32),
            pltpu.SemaphoreType.DMA((9,)),
        ],
    )
    got = lax.all_to_all(packed, "det", 0, 0, tiled=True)
    projected, labels = call(
        couple_kernel,
        (
            jax.ShapeDtypeStruct((PEERS, 2 * DETS, INNER), f32),
            jax.ShapeDtypeStruct((PEERS, 8, INNER), f32),
        ),
        [VMEM, HBM],
        got, coupling,
        scratch=[VMEM((MODES, MODES), f32), pltpu.SemaphoreType.DMA],
    )
    back = lax.all_to_all(projected, "det", 0, 0, tiled=True)
    twice = 2.0 * polar_angle[0]
    partials = call(
        bin_kernel,
        jax.ShapeDtypeStruct((2 * PEERS, ROWS, INNER), f32),
        [HBM] * 2 + [VMEM] * 5 + [HBM] * 3,
        device_slots, strip_tile, packed, weight, back, jnp.cos(twice), jnp.sin(twice),
        pixel_index, rows, inverse,
        scratch=[
            VMEM((OUTER * DETS, 2 * INNER), f32),
            VMEM((STRIPS, DETS, INNER), f32),
            SMEM((1, PEERS), jnp.int32),
            SMEM((DETS, STRIPS), jnp.int32),
            VMEM((DETS, 2 * SAMPLES), jnp.int32),
            VMEM((4 * OUTER, INNER), f32),
            VMEM((2, 2 * INNER, 2 * INNER), jnp.bfloat16),
            SMEM((PEERS,), jnp.int32),
            VMEM((UNROLL * 8 * DETS, INNER), f32),
            VMEM((PEERS, 2 * ROWS, INNER // 2), f32),
            VMEM((PEERS, 2 * ROWS, INNER // 2), f32),
            pltpu.SemaphoreType.DMA((5,)),
        ],
    )
    parts = lax.all_to_all(
        partials.reshape(PEERS, 2 * ROWS, INNER), "det", 0, 0, tiled=True
    )
    owned = call(
        gather_kernel,
        jax.ShapeDtypeStruct((2 * TM, ROWS + 8, INNER), f32),
        [SMEM] + [VMEM] * 2,
        slot_home, parts, labels,
    )
    final = lax.all_to_all(
        owned.reshape(TM, 2 * (ROWS + 8), INNER), "tm", 0, 0, tiled=True
    )
    placed = call(
        place_kernel,
        jax.ShapeDtypeStruct((3, OWN, 16 * INNER), f32),
        [VMEM],
        final.reshape(2 * TM, ROWS + 8, INNER),
        scratch=[VMEM((OWN * ROWS, INNER), f32)],
    )
    return placed.transpose(1, 0, 2)


def solution(mesh):
    strips = P("tm", "det", None)
    dets = P("tm", "det")
    return jax.shard_map(
        per_device,
        mesh=mesh,
        in_specs=(strips,) * 4 + (dets,) * 4 + (strips, P(), dets, dets),
        out_specs=P(("tm", "det"), None, None),
        check_vma=False,
    )
```

```python
import math

import jax
import jax.numpy as jnp
import numpy as np
from jax import lax
from jax.experimental import pallas as pl
from jax.experimental.pallas import tpu as pltpu
from jax.sharding import PartitionSpec as P

SAMPLES = 4096
OUTER = 32
INNER = 128
DETS = 16
PEERS = 32
STRIPS = 64
MODES = 64
TM = 4
OWN = 8
UNROLL = 8
HOT = 8
ROWS = 48

HIGHEST = lax.Precision.HIGHEST
VMEM = pltpu.VMEM
SMEM = pltpu.SMEM
HBM = pltpu.HBM


def tables():
    outer = np.arange(OUTER)[:, None]
    inner = np.arange(INNER)[None, :]
    twist = 2.0 * math.pi * outer * inner / SAMPLES
    grid = 2.0 * math.pi * np.outer(np.arange(INNER), np.arange(INNER)) / INNER
    cos_in, sin_in = np.cos(grid), np.sin(grid)
    forward = np.block([[cos_in, -sin_in], [sin_in, cos_in]])
    inverse = np.block([[cos_in, sin_in], [-sin_in, cos_in]]) / SAMPLES
    index = outer + OUTER * inner
    signed = (index + SAMPLES // 2) % SAMPLES - SAMPLES // 2
    freq = signed / SAMPLES
    log_freq = np.where(signed == 0, -1e30, np.log(np.maximum(np.abs(freq), 1e-9)))
    lag = np.where(signed == -(SAMPLES // 2), 0.0, 2.0 * math.pi * freq)
    rows = np.concatenate([np.cos(twist), np.sin(twist), log_freq, lag], axis=0)
    rows, forward, inverse = [np.asarray(t, np.float32) for t in (rows, forward, inverse)]
    top = inverse.astype(jnp.bfloat16)
    rest = (inverse - top.astype(np.float32)).astype(jnp.bfloat16)
    return rows, forward, np.stack([top, rest])


def transform(points, sign):
    count = len(points)
    if count == 1:
        return points
    even = transform(points[0::2], sign)
    odd = transform(points[1::2], sign)
    first, second = [], []
    half = count // 2
    for k in range(half):
        re, im = odd[k]
        angle = sign * 2.0 * math.pi * k / count
        c, s = math.cos(angle), math.sin(angle)
        if k == 0:
            tr, ti = re, im
        elif 4 * k == count:
            tr, ti = (-im, re) if sign > 0 else (im, -re)
        else:
            tr, ti = c * re - s * im, c * im + s * re
        er, ei = even[k]
        first.append((er + tr, ei + ti))
        second.append((er - tr, ei - ti))
    return first + second


def split(x):
    top = x.astype(jnp.bfloat16)
    return top, (x - top.astype(jnp.float32)).astype(jnp.bfloat16)


def product(left, right, dims=(((1,), (0,)), ((), ()))):
    def dot(a, b):
        return lax.dot_general(a, b, dims, preferred_element_type=jnp.float32)

    return dot(left[0], right[0]) + (dot(left[0], right[1]) + dot(left[1], right[0]))


def column(row):
    rows = lax.broadcasted_iota(jnp.int32, (DETS, DETS), 0)
    cols = lax.broadcasted_iota(jnp.int32, (DETS, DETS), 1)
    return jnp.sum(jnp.where(rows == cols, row, 0.0), axis=1, keepdims=True)


def ranks(slots, counts, mark):
    for block in range(PEERS):
        counts[block] = 0
    for entry in range(PEERS):
        slot = slots[0, entry]
        block = slot >> 2
        rank = counts[block]
        counts[block] = rank + 1
        mark(entry, slot, block, rank)


def forward_kernel(
    slots_h, signal_h, tau_h, knee_h, slope_h, white_h, mix_h, rows_h, matrix_h,
    out, scratch, slots, signal, tau, knee, slope, white, mix, rows, matrix,
    counts, sems,
):
    pairs = [
        (signal_h.at[0], signal), (rows_h, rows), (slots_h, slots), (tau_h, tau),
        (knee_h, knee), (slope_h, slope), (white_h, white), (mix_h.at[0], mix),
        (matrix_h, matrix),
    ]
    copies = [pltpu.make_async_copy(a, b, sems.at[i]) for i, (a, b) in enumerate(pairs)]
    for copy in copies:
        copy.start()
    for copy in copies[2:8]:
        copy.wait()
    mixed = jnp.concatenate([mix[0:8, :], mix[8:16, :]], axis=1)
    for k in range(OUTER):
        out[k, 32:40, :] = mixed
        out[k, 40:48, :] = jnp.full((8, INNER), -1.0, jnp.float32)

    def mark(entry, slot, block, rank):
        value = (slot - 4 * block).astype(jnp.float32)
        out[block, pl.ds(40 + rank, 1), :] = jnp.broadcast_to(value, (1, INNER))

    ranks(slots, counts, mark)
    for copy in copies[0:2]:
        copy.wait()
    for half in range(2):
        lo = 8 * half
        points = [
            (
                signal[lo : lo + 8, a * INNER : (a + 1) * INNER],
                signal[lo : lo + 8, (OUTER + a) * INNER : (OUTER + a + 1) * INNER],
            )
            for a in range(OUTER)
        ]
        for k, (re, im) in enumerate(transform(points, -1)):
            c = rows[k : k + 1, :]
            s = rows[OUTER + k : OUTER + k + 1, :]
            scratch[k * DETS + lo : k * DETS + lo + 8, 0:INNER] = re * c + im * s
            scratch[k * DETS + lo : k * DETS + lo + 8, INNER : 2 * INNER] = im * c - re * s
    tau_c, knee_p, slope_c, white_c = noise_params(tau, knee, slope, white)
    copies[8].wait()
    group = 8
    for start in range(0, OUTER, group):
        spec = jnp.dot(
            scratch[start * DETS : (start + group) * DETS, :],
            matrix[...],
            precision=HIGHEST,
            preferred_element_type=jnp.float32,
        )
        for step in range(group):
            k = start + step
            power = jnp.exp(slope_c * rows[2 * OUTER + k : 2 * OUTER + k + 1, :])
            weight = white_c * power / (power + knee_p)
            lag = tau_c * rows[3 * OUTER + k : 3 * OUTER + k + 1, :]
            re = spec[step * DETS : (step + 1) * DETS, 0:INNER]
            im = spec[step * DETS : (step + 1) * DETS, INNER : 2 * INNER]
            out[k, 0:DETS, :] = weight * (re - lag * im)
            out[k, DETS : 2 * DETS, :] = weight * (im + lag * re)


def couple_kernel(got, coupling_h, out, labels, coupling, sem):
    copy = pltpu.make_async_copy(coupling_h, coupling, sem)
    copy.start()
    amps = None
    mixes = []
    for half in range(2):
        lo = 8 * half
        re = got[:, lo : lo + 8, :].reshape(PEERS * 8, INNER)
        im = got[:, DETS + lo : DETS + lo + 8, :].reshape(PEERS * 8, INNER)
        mix = split(
            got[:, 32:40, half * MODES : (half + 1) * MODES].reshape(PEERS * 8, MODES)
        )
        both = split(jnp.concatenate([re, im], axis=1))
        part = product(mix, both, (((0,), (0,)), ((), ())))
        amps = part if amps is None else amps + part
        mixes.append(mix)
    copy.wait()
    coupled = split(product(split(coupling[...]), split(amps)))
    for half in range(2):
        lo = 8 * half
        back = product(mixes[half], coupled)
        out[:, lo : lo + 8, :] = back[:, 0:INNER].reshape(PEERS, 8, INNER)
        out[:, DETS + lo : DETS + lo + 8, :] = back[:, INNER:].reshape(PEERS, 8, INNER)
    labels[...] = got[:, 40:48, :]


def lane_marks():
    lanes = lax.broadcasted_iota(jnp.int32, (INNER, INNER), 1).astype(jnp.float32)
    return (
        lanes.astype(jnp.bfloat16),
        jnp.ones((INNER, INNER), jnp.bfloat16),
        jnp.zeros((INNER, INNER), jnp.bfloat16),
    )


def noise_params(tau, knee, slope, white):
    def wide(ref):
        return jnp.broadcast_to(column(ref[...]), (DETS, INNER))

    slope_c = wide(slope)
    return wide(tau), jnp.exp(slope_c * jnp.log(wide(knee))), slope_c, wide(white)


def hot_kernel(pixel, knee, slope, white, log_f, hot, lows, weight):
    lanes, one, none = lane_marks()
    pieces = [pixel[0, :, i * INNER : (i + 1) * INNER] & 127 for i in range(UNROLL)]
    turned = jnp.concatenate(pieces, axis=0).astype(jnp.float32).T
    lows[0] = turned
    for step in range(UNROLL):
        for d in range(0, DETS, HOT):
            at = step * DETS + d
            low_d = jnp.broadcast_to(turned[:, at : at + 1], (INNER, INNER))
            hot[0, at // HOT] = jnp.where(low_d.astype(jnp.bfloat16) == lanes, one, none)
    _, knee_p, slope_c, white_c = noise_params(knee, knee, slope, white)
    for k in range(weight.shape[0]):
        power = jnp.exp(slope_c * log_f[0, k : k + 1, :])
        weight[k] = white_c * power / (power + knee_p)


def bin_kernel(
    slots_h, tiles_h, weighted, weight, back, cosine, sine, pixel_h, rows_h, matrix_h,
    lows_h, hot_h, out, scratch, stream, slots, tiles, pixel, rows, matrix, counts, parts,
    even, odd, hot, lows, sems, hot_sems, low_sems,
):
    pairs = [
        (matrix_h, matrix), (rows_h, rows), (slots_h, slots), (tiles_h.at[0], tiles),
        (pixel_h.at[0], pixel),
    ]
    copies = [pltpu.make_async_copy(a, b, sems.at[i]) for i, (a, b) in enumerate(pairs)]
    for copy in copies:
        copy.start()

    def load(start, slot):
        return (
            pltpu.make_async_copy(hot_h.at[start], hot.at[slot], hot_sems.at[slot]),
            pltpu.make_async_copy(lows_h.at[start], lows.at[slot], low_sems.at[slot]),
        )

    for copy in load(0, 0):
        copy.start()
    for k in range(OUTER):
        re = weighted[k, 0:DETS, :] - weight[k] * back[k, 0:DETS, :]
        im = weighted[k, DETS : 2 * DETS, :] - weight[k] * back[k, DETS : 2 * DETS, :]
        scratch[k * DETS : (k + 1) * DETS, 0:INNER] = re
        scratch[k * DETS : (k + 1) * DETS, INNER : 2 * INNER] = im
    for copy in copies[0:2]:
        copy.wait()
    group = 8
    for start in range(0, OUTER, group):
        section = product(
            split(scratch[start * DETS : (start + group) * DETS, :]), (matrix[0], matrix[1])
        )
        for step in range(group):
            k = start + step
            c = rows[k : k + 1, :]
            s = rows[OUTER + k : OUTER + k + 1, :]
            re = section[step * DETS : (step + 1) * DETS, 0:INNER]
            im = section[step * DETS : (step + 1) * DETS, INNER : 2 * INNER]
            scratch[k * DETS : (k + 1) * DETS, 0:INNER] = re * c - im * s
            scratch[k * DETS : (k + 1) * DETS, INNER : 2 * INNER] = im * c + re * s
    for half in range(2):
        lo = 8 * half
        points = [
            (
                scratch[k * DETS + lo : k * DETS + lo + 8, 0:INNER],
                scratch[k * DETS + lo : k * DETS + lo + 8, INNER : 2 * INNER],
            )
            for k in range(OUTER)
        ]
        for a, (re, im) in enumerate(transform(points, 1)):
            stream[a, lo : lo + 8, :] = re
            stream[OUTER + a, lo : lo + 8, :] = im

    def clear(entry, carry):
        blank = jnp.zeros((ROWS, INNER), jnp.float32)
        even[entry] = blank
        odd[entry] = blank
        out[entry] = blank
        out[PEERS + entry] = blank
        return carry

    lax.fori_loop(0, PEERS, clear, 0)
    for copy in copies[2:]:
        copy.wait()
    levels = (lax.broadcasted_iota(jnp.int32, (16, INNER), 0) & 7).astype(jnp.float32)
    marks = [(levels + 8.0 * g).astype(jnp.bfloat16) for g in range(2)]
    zero = jnp.zeros((16, INNER), jnp.bfloat16)
    lanes, one, none = lane_marks()

    def block(start, carry):
        slot = start & 1
        for copy in load(start, slot):
            copy.wait()

        @pl.when(start + 1 < STRIPS // UNROLL)
        def _():
            for copy in load(start + 1, 1 - slot):
                copy.start()

        for step in range(UNROLL):
            s = start * UNROLL + step
            base = pl.multiple_of(s * INNER, INNER)
            pix = pixel[:, pl.ds(base, INNER)]
            values = stream[s]
            maps = [
                values,
                values * cosine[:, pl.ds(base, INNER)],
                values * sine[:, pl.ds(base, INNER)],
            ]
            tops = [m.astype(jnp.bfloat16).astype(jnp.float32) for m in maps]
            rests = [m - t for m, t in zip(maps, tops)]
            for i, field in enumerate([(pix >> 7).astype(jnp.float32)] + tops + rests):
                at = (step * 7 + i) * DETS
                parts[at : at + DETS, :] = field
        for step in range(UNROLL):
            s = start * UNROLL + step

            def spread(i, j, d):
                lines = [
                    parts[pl.ds((step * 7 + n) * DETS + d, 8, stride=0), :] for n in (i, j)
                ]
                return jnp.concatenate(lines, axis=0).astype(jnp.bfloat16)

            for d in range(DETS):
                at = step * DETS + d
                high_d = spread(0, 0, d)
                hits = [high_d == mark for mark in marks]
                left = []
                for c in range(3):
                    both = spread(1 + c, 4 + c, d)
                    left += [jnp.where(hit, both, zero) for hit in hits]
                left = jnp.concatenate(left, axis=0)
                if d % HOT == 0:
                    right = hot[slot, at // HOT]
                else:
                    low_d = jnp.broadcast_to(lows[slot, :, at : at + 1], (INNER, INNER))
                    right = jnp.where(low_d.astype(jnp.bfloat16) == lanes, one, none)
                sums = jnp.dot(left, right, preferred_element_type=jnp.float32)
                tile = tiles[d, s]
                total = (even, odd)[d % 2]
                sums = sums.reshape(6, 2, 8, INNER)
                total[tile] = total[tile] + (sums[:, 0] + sums[:, 1]).reshape(ROWS, INNER)
        return carry

    lax.fori_loop(0, STRIPS // UNROLL, block, 0)

    def settle(entry, slot, home, rank):
        out[2 * home + rank] = even[entry] + odd[entry]

    ranks(slots, counts, settle)


def gather_kernel(homes, got, labels, out):
    for place in range(2 * TM):
        out[place, 0:ROWS, :] = jnp.zeros((ROWS, INNER), jnp.float32)
        out[place, ROWS:, :] = jnp.full((8, INNER), -1.0, jnp.float32)
    for tile in range(4):
        def add(source, total):
            for rank in range(2):
                hit = labels[source, rank : rank + 1, :] == float(tile)
                total = total + jnp.where(
                    hit, got[source, rank * ROWS : (rank + 1) * ROWS, :], 0.0
                )
            return total

        total = lax.fori_loop(
            0, PEERS, add, jnp.zeros((ROWS, INNER), jnp.float32), unroll=4
        )
        owner = homes[0, tile] // OWN
        rank = 0
        for other in range(tile):
            rank = rank + jnp.where(homes[0, other] // OWN == owner, 1, 0)
        row = 2 * owner + rank
        out[row, 0:ROWS, :] = total
        place = (homes[0, tile] - OWN * owner).astype(jnp.float32)
        out[row, ROWS:, :] = jnp.broadcast_to(place, (8, INNER))


def place_kernel(got, out, totals):
    for place in range(OWN):
        total = jnp.zeros((ROWS, INNER), jnp.float32)
        for source in range(2 * TM):
            hit = got[source, ROWS : ROWS + 1, :] == float(place)
            total = total + jnp.where(hit, got[source, 0:ROWS, :], 0.0)
        totals[place * ROWS : (place + 1) * ROWS, :] = total
    for row in range(ROWS):
        at = (row % 16) * INNER
        out[row // 16, :, at : at + INNER] = totals[pl.ds(row, OWN, stride=ROWS), :]


def call(kernel, outs, specs, *operands, scratch=()):
    operands = [
        pltpu.with_memory_space_constraint(o, HBM) if m is HBM else o
        for o, m in zip(operands, specs)
    ]
    return pl.pallas_call(
        kernel,
        out_shape=outs,
        in_specs=[pl.BlockSpec(memory_space=s) for s in specs],
        scratch_shapes=list(scratch),
        compiler_params=pltpu.CompilerParams(vmem_limit_bytes=9 << 20),
    )(*operands)


def per_device(
    timestream, polar_angle, pixel_index, strip_tile, time_const, knee_freq, noise_slope,
    white_weight, mode_mix, coupling, device_slots, slot_home,
):
    f32 = jnp.float32
    table, forward, inverse = tables()
    rows, forward, inverse = [jnp.asarray(t) for t in (table, forward, inverse)]
    packed = call(
        forward_kernel,
        jax.ShapeDtypeStruct((PEERS, 48, INNER), f32),
        [HBM] * 9,
        device_slots, timestream, time_const, knee_freq, noise_slope, white_weight,
        mode_mix, rows, forward,
        scratch=[
            VMEM((OUTER * DETS, 2 * INNER), f32),
            SMEM((1, PEERS), jnp.int32),
            VMEM((DETS, 2 * SAMPLES), f32),
            VMEM((1, DETS), f32),
            VMEM((1, DETS), f32),
            VMEM((1, DETS), f32),
            VMEM((1, DETS), f32),
            VMEM((DETS, MODES), f32),
            VMEM((4 * OUTER, INNER), f32),
            VMEM((2 * INNER, 2 * INNER), f32),
            SMEM((PEERS,), jnp.int32),
            pltpu.SemaphoreType.DMA((9,)),
        ],
    )
    got = lax.all_to_all(packed, "det", 0, 0, tiled=True)
    projected, labels = call(
        couple_kernel,
        (
            jax.ShapeDtypeStruct((PEERS, 2 * DETS, INNER), f32),
            jax.ShapeDtypeStruct((PEERS, 8, INNER), f32),
        ),
        [VMEM, HBM],
        got, coupling,
        scratch=[VMEM((MODES, MODES), f32), pltpu.SemaphoreType.DMA],
    )
    back = lax.all_to_all(projected, "det", 0, 0, tiled=True)
    blocks = STRIPS // UNROLL
    width = UNROLL * INNER
    halves = UNROLL * DETS // HOT
    ks = OUTER // blocks
    hot, lows, weight = pl.pallas_call(
        hot_kernel,
        out_shape=(
            HBM((blocks, halves, INNER, INNER), jnp.bfloat16),
            HBM((blocks, INNER, UNROLL * DETS), f32),
            jax.ShapeDtypeStruct((OUTER, DETS, INNER), f32),
        ),
        grid=(blocks,),
        in_specs=[pl.BlockSpec((1, DETS, width), lambda i: (0, 0, i))]
        + [pl.BlockSpec((1, DETS), lambda i: (0, 0))] * 3
        + [pl.BlockSpec((1, ks, INNER), lambda i: (i, 0, 0))],
        out_specs=(
            pl.BlockSpec((1, halves, INNER, INNER), lambda i: (i, 0, 0, 0)),
            pl.BlockSpec((1, INNER, UNROLL * DETS), lambda i: (i, 0, 0)),
            pl.BlockSpec((ks, DETS, INNER), lambda i: (i, 0, 0)),
        ),
        compiler_params=pltpu.CompilerParams(vmem_limit_bytes=9 << 20),
    )(
        pixel_index, knee_freq, noise_slope, white_weight,
        jnp.asarray(table[2 * OUTER : 3 * OUTER].reshape(blocks, ks, INNER)),
    )
    twice = 2.0 * polar_angle[0]
    partials = call(
        bin_kernel,
        jax.ShapeDtypeStruct((2 * PEERS, ROWS, INNER), f32),
        [HBM] * 2 + [VMEM] * 5 + [HBM] * 5,
        device_slots, strip_tile, packed, weight, back, jnp.cos(twice), jnp.sin(twice),
        pixel_index, rows, inverse, lows, hot,
        scratch=[
            VMEM((OUTER * DETS, 2 * INNER), f32),
            VMEM((STRIPS, DETS, INNER), f32),
            SMEM((1, PEERS), jnp.int32),
            SMEM((DETS, STRIPS), jnp.int32),
            VMEM((DETS, 2 * SAMPLES), jnp.int32),
            VMEM((4 * OUTER, INNER), f32),
            VMEM((2, 2 * INNER, 2 * INNER), jnp.bfloat16),
            SMEM((PEERS,), jnp.int32),
            VMEM((UNROLL * 7 * DETS, INNER), f32),
            VMEM((PEERS, ROWS, INNER), f32),
            VMEM((PEERS, ROWS, INNER), f32),
            VMEM((2, UNROLL * DETS // HOT, INNER, INNER), jnp.bfloat16),
            VMEM((2, INNER, UNROLL * DETS), f32),
            pltpu.SemaphoreType.DMA((5,)),
            pltpu.SemaphoreType.DMA((2,)),
            pltpu.SemaphoreType.DMA((2,)),
        ],
    )
    parts = lax.all_to_all(
        partials.reshape(PEERS, 2 * ROWS, INNER), "det", 0, 0, tiled=True
    )
    owned = call(
        gather_kernel,
        jax.ShapeDtypeStruct((2 * TM, ROWS + 8, INNER), f32),
        [SMEM] + [VMEM] * 2,
        slot_home, parts, labels,
    )
    final = lax.all_to_all(
        owned.reshape(TM, 2 * (ROWS + 8), INNER), "tm", 0, 0, tiled=True
    )
    placed = call(
        place_kernel,
        jax.ShapeDtypeStruct((3, OWN, 16 * INNER), f32),
        [VMEM],
        final.reshape(2 * TM, ROWS + 8, INNER),
        scratch=[VMEM((OWN * ROWS, INNER), f32)],
    )
    return placed.transpose(1, 0, 2)


def solution(mesh):
    strips = P("tm", "det", None)
    dets = P("tm", "det")
    return jax.shard_map(
        per_device,
        mesh=mesh,
        in_specs=(strips,) * 4 + (dets,) * 4 + (strips, P(), dets, dets),
        out_specs=P(("tm", "det"), None, None),
        check_vma=False,
    )
```

```python
import math

import jax
import jax.numpy as jnp
import numpy as np
from jax import lax
from jax.experimental import pallas as pl
from jax.experimental.pallas import tpu as pltpu
from jax.sharding import PartitionSpec as P

SAMPLES = 4096
OUTER = 32
INNER = 128
DETS = 16
PEERS = 32
STRIPS = 64
MODES = 64
TM = 4
OWN = 8
UNROLL = 8
HOT = 8
ROWS = 48

HIGHEST = lax.Precision.HIGHEST
VMEM = pltpu.VMEM
SMEM = pltpu.SMEM
HBM = pltpu.HBM


def tables():
    outer = np.arange(OUTER)[:, None]
    inner = np.arange(INNER)[None, :]
    twist = 2.0 * math.pi * outer * inner / SAMPLES
    grid = 2.0 * math.pi * np.outer(np.arange(INNER), np.arange(INNER)) / INNER
    cos_in, sin_in = np.cos(grid), np.sin(grid)
    forward = np.block([[cos_in, -sin_in], [sin_in, cos_in]])
    inverse = np.block([[cos_in, sin_in], [-sin_in, cos_in]]) / SAMPLES
    index = outer + OUTER * inner
    signed = (index + SAMPLES // 2) % SAMPLES - SAMPLES // 2
    freq = signed / SAMPLES
    log_freq = np.where(signed == 0, -1e30, np.log(np.maximum(np.abs(freq), 1e-9)))
    lag = np.where(signed == -(SAMPLES // 2), 0.0, 2.0 * math.pi * freq)
    rows = np.concatenate([np.cos(twist), np.sin(twist), log_freq, lag], axis=0)
    rows, forward, inverse = [np.asarray(t, np.float32) for t in (rows, forward, inverse)]
    top = inverse.astype(jnp.bfloat16)
    rest = (inverse - top.astype(np.float32)).astype(jnp.bfloat16)
    return rows, forward, np.stack([top, rest])


def transform(points, sign):
    count = len(points)
    if count == 1:
        return points
    even = transform(points[0::2], sign)
    odd = transform(points[1::2], sign)
    first, second = [], []
    half = count // 2
    for k in range(half):
        re, im = odd[k]
        angle = sign * 2.0 * math.pi * k / count
        c, s = math.cos(angle), math.sin(angle)
        if k == 0:
            tr, ti = re, im
        elif 4 * k == count:
            tr, ti = (-im, re) if sign > 0 else (im, -re)
        else:
            tr, ti = c * re - s * im, c * im + s * re
        er, ei = even[k]
        first.append((er + tr, ei + ti))
        second.append((er - tr, ei - ti))
    return first + second


def split(x):
    top = x.astype(jnp.bfloat16)
    return top, (x - top.astype(jnp.float32)).astype(jnp.bfloat16)


def product(left, right, dims=(((1,), (0,)), ((), ()))):
    def dot(a, b):
        return lax.dot_general(a, b, dims, preferred_element_type=jnp.float32)

    return dot(left[0], right[0]) + (dot(left[0], right[1]) + dot(left[1], right[0]))


def column(row):
    rows = lax.broadcasted_iota(jnp.int32, (DETS, DETS), 0)
    cols = lax.broadcasted_iota(jnp.int32, (DETS, DETS), 1)
    return jnp.sum(jnp.where(rows == cols, row, 0.0), axis=1, keepdims=True)


def ranks(slots, counts, mark):
    for block in range(PEERS):
        counts[block] = 0
    for entry in range(PEERS):
        slot = slots[0, entry]
        block = slot >> 2
        rank = counts[block]
        counts[block] = rank + 1
        mark(entry, slot, block, rank)


def forward_kernel(
    slots_h, signal_h, tau_h, knee_h, slope_h, white_h, mix_h, rows_h, matrix_h,
    out, scratch, slots, signal, tau, knee, slope, white, mix, rows, matrix,
    counts, sems,
):
    pairs = [
        (signal_h.at[0], signal), (rows_h, rows), (slots_h, slots), (tau_h, tau),
        (knee_h, knee), (slope_h, slope), (white_h, white), (mix_h.at[0], mix),
        (matrix_h, matrix),
    ]
    copies = [pltpu.make_async_copy(a, b, sems.at[i]) for i, (a, b) in enumerate(pairs)]
    for copy in copies:
        copy.start()
    for copy in copies[2:8]:
        copy.wait()
    mixed = jnp.concatenate([mix[0:8, :], mix[8:16, :]], axis=1)
    for k in range(OUTER):
        out[k, 32:40, :] = mixed
        out[k, 40:48, :] = jnp.full((8, INNER), -1.0, jnp.float32)

    def mark(entry, slot, block, rank):
        value = (slot - 4 * block).astype(jnp.float32)
        out[block, pl.ds(40 + rank, 1), :] = jnp.broadcast_to(value, (1, INNER))

    ranks(slots, counts, mark)
    for copy in copies[0:2]:
        copy.wait()
    for half in range(2):
        lo = 8 * half
        points = [
            (
                signal[lo : lo + 8, a * INNER : (a + 1) * INNER],
                signal[lo : lo + 8, (OUTER + a) * INNER : (OUTER + a + 1) * INNER],
            )
            for a in range(OUTER)
        ]
        for k, (re, im) in enumerate(transform(points, -1)):
            c = rows[k : k + 1, :]
            s = rows[OUTER + k : OUTER + k + 1, :]
            scratch[k * DETS + lo : k * DETS + lo + 8, 0:INNER] = re * c + im * s
            scratch[k * DETS + lo : k * DETS + lo + 8, INNER : 2 * INNER] = im * c - re * s
    tau_c, knee_p, slope_c, white_c = noise_params(tau, knee, slope, white)
    copies[8].wait()
    group = 8
    for start in range(0, OUTER, group):
        spec = jnp.dot(
            scratch[start * DETS : (start + group) * DETS, :],
            matrix[...],
            precision=HIGHEST,
            preferred_element_type=jnp.float32,
        )
        for step in range(group):
            k = start + step
            power = jnp.exp(slope_c * rows[2 * OUTER + k : 2 * OUTER + k + 1, :])
            weight = white_c * power / (power + knee_p)
            lag = tau_c * rows[3 * OUTER + k : 3 * OUTER + k + 1, :]
            re = spec[step * DETS : (step + 1) * DETS, 0:INNER]
            im = spec[step * DETS : (step + 1) * DETS, INNER : 2 * INNER]
            out[k, 0:DETS, :] = weight * (re - lag * im)
            out[k, DETS : 2 * DETS, :] = weight * (im + lag * re)


def couple_kernel(got, coupling_h, out, labels, coupling, sem):
    copy = pltpu.make_async_copy(coupling_h, coupling, sem)
    copy.start()
    amps = None
    mixes = []
    for half in range(2):
        lo = 8 * half
        re = got[:, lo : lo + 8, :].reshape(PEERS * 8, INNER)
        im = got[:, DETS + lo : DETS + lo + 8, :].reshape(PEERS * 8, INNER)
        mix = split(
            got[:, 32:40, half * MODES : (half + 1) * MODES].reshape(PEERS * 8, MODES)
        )
        both = split(jnp.concatenate([re, im], axis=1))
        part = product(mix, both, (((0,), (0,)), ((), ())))
        amps = part if amps is None else amps + part
        mixes.append(mix)
    copy.wait()
    coupled = split(product(split(coupling[...]), split(amps)))
    for half in range(2):
        lo = 8 * half
        back = product(mixes[half], coupled)
        out[:, lo : lo + 8, :] = back[:, 0:INNER].reshape(PEERS, 8, INNER)
        out[:, DETS + lo : DETS + lo + 8, :] = back[:, INNER:].reshape(PEERS, 8, INNER)
    labels[...] = got[:, 40:48, :]


def lane_marks():
    lanes = lax.broadcasted_iota(jnp.int32, (INNER, INNER), 1).astype(jnp.float32)
    return (
        lanes.astype(jnp.bfloat16),
        jnp.ones((INNER, INNER), jnp.bfloat16),
        jnp.zeros((INNER, INNER), jnp.bfloat16),
    )


def noise_params(tau, knee, slope, white):
    def wide(ref):
        return jnp.broadcast_to(column(ref[...]), (DETS, INNER))

    slope_c = wide(slope)
    return wide(tau), jnp.exp(slope_c * jnp.log(wide(knee))), slope_c, wide(white)


def hot_kernel(pixel, knee, slope, white, log_f, hot, lows, weight):
    lanes, one, none = lane_marks()
    pieces = [pixel[0, :, i * INNER : (i + 1) * INNER] & 127 for i in range(UNROLL)]
    turned = jnp.concatenate(pieces, axis=0).astype(jnp.float32).T
    lows[0] = turned
    for step in range(UNROLL):
        for d in range(0, DETS, HOT):
            at = step * DETS + d
            low_d = jnp.broadcast_to(turned[:, at : at + 1], (INNER, INNER))
            hot[0, at // HOT] = jnp.where(low_d.astype(jnp.bfloat16) == lanes, one, none)
    _, knee_p, slope_c, white_c = noise_params(knee, knee, slope, white)
    for k in range(weight.shape[0]):
        power = jnp.exp(slope_c * log_f[0, k : k + 1, :])
        weight[k] = white_c * power / (power + knee_p)


def bin_kernel(
    slots_h, tiles_h, weighted, weight, back, cosine, sine, pixel_h, rows_h, matrix_h,
    lows_h, hot_h, out, scratch, stream, slots, tiles, pixel, rows, matrix, counts, parts,
    even, odd, hot, lows, sems, hot_sems, low_sems,
):
    pairs = [
        (matrix_h, matrix), (rows_h, rows), (slots_h, slots), (tiles_h.at[0], tiles),
        (pixel_h.at[0], pixel),
    ]
    copies = [pltpu.make_async_copy(a, b, sems.at[i]) for i, (a, b) in enumerate(pairs)]
    for copy in copies:
        copy.start()

    def load(start, slot):
        return (
            pltpu.make_async_copy(hot_h.at[start], hot.at[slot], hot_sems.at[slot]),
            pltpu.make_async_copy(lows_h.at[start], lows.at[slot], low_sems.at[slot]),
        )

    for copy in load(0, 0):
        copy.start()
    def clear(entry, carry):
        blank = jnp.zeros((ROWS, INNER), jnp.float32)
        even[entry] = blank
        odd[entry] = blank
        out[entry] = blank
        out[PEERS + entry] = blank
        return carry

    lax.fori_loop(0, PEERS, clear, 0)
    for k in range(OUTER):
        re = weighted[k, 0:DETS, :] - weight[k] * back[k, 0:DETS, :]
        im = weighted[k, DETS : 2 * DETS, :] - weight[k] * back[k, DETS : 2 * DETS, :]
        scratch[k * DETS : (k + 1) * DETS, 0:INNER] = re
        scratch[k * DETS : (k + 1) * DETS, INNER : 2 * INNER] = im
    for copy in copies[0:2]:
        copy.wait()
    group = 8
    for start in range(0, OUTER, group):
        section = product(
            split(scratch[start * DETS : (start + group) * DETS, :]), (matrix[0], matrix[1])
        )
        for step in range(group):
            k = start + step
            c = rows[k : k + 1, :]
            s = rows[OUTER + k : OUTER + k + 1, :]
            re = section[step * DETS : (step + 1) * DETS, 0:INNER]
            im = section[step * DETS : (step + 1) * DETS, INNER : 2 * INNER]
            scratch[k * DETS : (k + 1) * DETS, 0:INNER] = re * c - im * s
            scratch[k * DETS : (k + 1) * DETS, INNER : 2 * INNER] = im * c + re * s
    for half in range(2):
        lo = 8 * half
        points = [
            (
                scratch[k * DETS + lo : k * DETS + lo + 8, 0:INNER],
                scratch[k * DETS + lo : k * DETS + lo + 8, INNER : 2 * INNER],
            )
            for k in range(OUTER)
        ]
        for a, (re, im) in enumerate(transform(points, 1)):
            stream[a, lo : lo + 8, :] = re
            stream[OUTER + a, lo : lo + 8, :] = im

    for copy in copies[2:]:
        copy.wait()
    levels = (lax.broadcasted_iota(jnp.int32, (16, INNER), 0) & 7).astype(jnp.float32)
    marks = [(levels + 8.0 * g).astype(jnp.bfloat16) for g in range(2)]
    zero = jnp.zeros((16, INNER), jnp.bfloat16)
    lanes, one, none = lane_marks()

    def block(start, carry):
        slot = start & 1
        for copy in load(start, slot):
            copy.wait()

        @pl.when(start + 1 < STRIPS // UNROLL)
        def _():
            for copy in load(start + 1, 1 - slot):
                copy.start()

        for step in range(UNROLL):
            s = start * UNROLL + step
            base = pl.multiple_of(s * INNER, INNER)
            pix = pixel[:, pl.ds(base, INNER)]
            values = stream[s]
            maps = [
                values,
                values * cosine[:, pl.ds(base, INNER)],
                values * sine[:, pl.ds(base, INNER)],
            ]
            tops = [m.astype(jnp.bfloat16).astype(jnp.float32) for m in maps]
            rests = [m - t for m, t in zip(maps, tops)]
            for i, field in enumerate([(pix >> 7).astype(jnp.float32)] + tops + rests):
                at = (step * 7 + i) * DETS
                parts[at : at + DETS, :] = field
        for step in range(UNROLL):
            s = start * UNROLL + step

            def spread(i, j, d):
                lines = [
                    parts[pl.ds((step * 7 + n) * DETS + d, 8, stride=0), :] for n in (i, j)
                ]
                return jnp.concatenate(lines, axis=0).astype(jnp.bfloat16)

            for d in range(DETS):
                at = step * DETS + d
                high_d = spread(0, 0, d)
                hits = [high_d == mark for mark in marks]
                left = []
                for c in range(3):
                    both = spread(1 + c, 4 + c, d)
                    left += [jnp.where(hit, both, zero) for hit in hits]
                left = jnp.concatenate(left, axis=0)
                if d % HOT == 0:
                    right = hot[slot, at // HOT]
                else:
                    low_d = jnp.broadcast_to(lows[slot, :, at : at + 1], (INNER, INNER))
                    right = jnp.where(low_d.astype(jnp.bfloat16) == lanes, one, none)
                sums = jnp.dot(left, right, preferred_element_type=jnp.float32)
                tile = tiles[d, s]
                total = (even, odd)[d % 2]
                sums = sums.reshape(6, 2, 8, INNER)
                total[tile] = total[tile] + (sums[:, 0] + sums[:, 1]).reshape(ROWS, INNER)
        return carry

    lax.fori_loop(0, STRIPS // UNROLL, block, 0)

    def settle(entry, slot, home, rank):
        out[2 * home + rank] = even[entry] + odd[entry]

    ranks(slots, counts, settle)


def gather_kernel(homes, got, labels, out):
    for place in range(2 * TM):
        out[place, 0:ROWS, :] = jnp.zeros((ROWS, INNER), jnp.float32)
        out[place, ROWS:, :] = jnp.full((8, INNER), -1.0, jnp.float32)
    def add(source, totals):
        totals = list(totals)
        for rank in range(2):
            slab = got[source, rank * ROWS : (rank + 1) * ROWS, :]
            label = labels[source, rank : rank + 1, :]
            for tile in range(4):
                totals[tile] = totals[tile] + jnp.where(label == float(tile), slab, 0.0)
        return tuple(totals)

    blank = jnp.zeros((ROWS, INNER), jnp.float32)
    totals = lax.fori_loop(0, PEERS, add, (blank,) * 4, unroll=4)
    for tile in range(4):
        total = totals[tile]
        owner = homes[0, tile] // OWN
        rank = 0
        for other in range(tile):
            rank = rank + jnp.where(homes[0, other] // OWN == owner, 1, 0)
        row = 2 * owner + rank
        out[row, 0:ROWS, :] = total
        place = (homes[0, tile] - OWN * owner).astype(jnp.float32)
        out[row, ROWS:, :] = jnp.broadcast_to(place, (8, INNER))


def place_kernel(got, out, totals):
    for place in range(OWN):
        total = jnp.zeros((ROWS, INNER), jnp.float32)
        for source in range(2 * TM):
            hit = got[source, ROWS : ROWS + 1, :] == float(place)
            total = total + jnp.where(hit, got[source, 0:ROWS, :], 0.0)
        totals[place * ROWS : (place + 1) * ROWS, :] = total
    for row in range(ROWS):
        at = (row % 16) * INNER
        out[row // 16, :, at : at + INNER] = totals[pl.ds(row, OWN, stride=ROWS), :]


def call(kernel, outs, specs, *operands, scratch=()):
    operands = [
        pltpu.with_memory_space_constraint(o, HBM) if m is HBM else o
        for o, m in zip(operands, specs)
    ]
    return pl.pallas_call(
        kernel,
        out_shape=outs,
        in_specs=[pl.BlockSpec(memory_space=s) for s in specs],
        scratch_shapes=list(scratch),
        compiler_params=pltpu.CompilerParams(vmem_limit_bytes=9 << 20),
    )(*operands)


def per_device(
    timestream, polar_angle, pixel_index, strip_tile, time_const, knee_freq, noise_slope,
    white_weight, mode_mix, coupling, device_slots, slot_home,
):
    f32 = jnp.float32
    table, forward, inverse = tables()
    rows, forward, inverse = [jnp.asarray(t) for t in (table, forward, inverse)]
    packed = call(
        forward_kernel,
        jax.ShapeDtypeStruct((PEERS, 48, INNER), f32),
        [HBM] * 9,
        device_slots, timestream, time_const, knee_freq, noise_slope, white_weight,
        mode_mix, rows, forward,
        scratch=[
            VMEM((OUTER * DETS, 2 * INNER), f32),
            SMEM((1, PEERS), jnp.int32),
            VMEM((DETS, 2 * SAMPLES), f32),
            VMEM((1, DETS), f32),
            VMEM((1, DETS), f32),
            VMEM((1, DETS), f32),
            VMEM((1, DETS), f32),
            VMEM((DETS, MODES), f32),
            VMEM((4 * OUTER, INNER), f32),
            VMEM((2 * INNER, 2 * INNER), f32),
            SMEM((PEERS,), jnp.int32),
            pltpu.SemaphoreType.DMA((9,)),
        ],
    )
    got = lax.all_to_all(packed, "det", 0, 0, tiled=True)
    projected, labels = call(
        couple_kernel,
        (
            jax.ShapeDtypeStruct((PEERS, 2 * DETS, INNER), f32),
            jax.ShapeDtypeStruct((PEERS, 8, INNER), f32),
        ),
        [VMEM, HBM],
        got, coupling,
        scratch=[VMEM((MODES, MODES), f32), pltpu.SemaphoreType.DMA],
    )
    back = lax.all_to_all(projected, "det", 0, 0, tiled=True)
    blocks = STRIPS // UNROLL
    width = UNROLL * INNER
    halves = UNROLL * DETS // HOT
    ks = OUTER // blocks
    hot, lows, weight = pl.pallas_call(
        hot_kernel,
        out_shape=(
            HBM((blocks, halves, INNER, INNER), jnp.bfloat16),
            HBM((blocks, INNER, UNROLL * DETS), f32),
            jax.ShapeDtypeStruct((OUTER, DETS, INNER), f32),
        ),
        grid=(blocks,),
        in_specs=[pl.BlockSpec((1, DETS, width), lambda i: (0, 0, i))]
        + [pl.BlockSpec((1, DETS), lambda i: (0, 0))] * 3
        + [pl.BlockSpec((1, ks, INNER), lambda i: (i, 0, 0))],
        out_specs=(
            pl.BlockSpec((1, halves, INNER, INNER), lambda i: (i, 0, 0, 0)),
            pl.BlockSpec((1, INNER, UNROLL * DETS), lambda i: (i, 0, 0)),
            pl.BlockSpec((ks, DETS, INNER), lambda i: (i, 0, 0)),
        ),
        compiler_params=pltpu.CompilerParams(vmem_limit_bytes=9 << 20),
    )(
        pixel_index, knee_freq, noise_slope, white_weight,
        jnp.asarray(table[2 * OUTER : 3 * OUTER].reshape(blocks, ks, INNER)),
    )
    twice = 2.0 * polar_angle[0]
    partials = call(
        bin_kernel,
        jax.ShapeDtypeStruct((2 * PEERS, ROWS, INNER), f32),
        [HBM] * 2 + [VMEM] * 5 + [HBM] * 5,
        device_slots, strip_tile, packed, weight, back, jnp.cos(twice), jnp.sin(twice),
        pixel_index, rows, inverse, lows, hot,
        scratch=[
            VMEM((OUTER * DETS, 2 * INNER), f32),
            VMEM((STRIPS, DETS, INNER), f32),
            SMEM((1, PEERS), jnp.int32),
            SMEM((DETS, STRIPS), jnp.int32),
            VMEM((DETS, 2 * SAMPLES), jnp.int32),
            VMEM((4 * OUTER, INNER), f32),
            VMEM((2, 2 * INNER, 2 * INNER), jnp.bfloat16),
            SMEM((PEERS,), jnp.int32),
            VMEM((UNROLL * 7 * DETS, INNER), f32),
            VMEM((PEERS, ROWS, INNER), f32),
            VMEM((PEERS, ROWS, INNER), f32),
            VMEM((2, UNROLL * DETS // HOT, INNER, INNER), jnp.bfloat16),
            VMEM((2, INNER, UNROLL * DETS), f32),
            pltpu.SemaphoreType.DMA((5,)),
            pltpu.SemaphoreType.DMA((2,)),
            pltpu.SemaphoreType.DMA((2,)),
        ],
    )
    parts = lax.all_to_all(
        partials.reshape(PEERS, 2 * ROWS, INNER), "det", 0, 0, tiled=True
    )
    owned = call(
        gather_kernel,
        jax.ShapeDtypeStruct((2 * TM, ROWS + 8, INNER), f32),
        [SMEM] + [VMEM] * 2,
        slot_home, parts, labels,
    )
    final = lax.all_to_all(
        owned.reshape(TM, 2 * (ROWS + 8), INNER), "tm", 0, 0, tiled=True
    )
    placed = call(
        place_kernel,
        jax.ShapeDtypeStruct((3, OWN, 16 * INNER), f32),
        [VMEM],
        final.reshape(2 * TM, ROWS + 8, INNER),
        scratch=[VMEM((OWN * ROWS, INNER), f32)],
    )
    return placed.transpose(1, 0, 2)


def solution(mesh):
    strips = P("tm", "det", None)
    dets = P("tm", "det")
    return jax.shard_map(
        per_device,
        mesh=mesh,
        in_specs=(strips,) * 4 + (dets,) * 4 + (strips, P(), dets, dets),
        out_specs=P(("tm", "det"), None, None),
        check_vma=False,
    )
```

```python
import math

import jax
import jax.numpy as jnp
import numpy as np
from jax import lax
from jax.experimental import pallas as pl
from jax.experimental.pallas import tpu as pltpu
from jax.sharding import PartitionSpec as P

SAMPLES = 4096
OUTER = 32
INNER = 128
DETS = 16
PEERS = 32
STRIPS = 64
MODES = 64
TM = 4
OWN = 8
UNROLL = 8
HOT = 8
ROWS = 48

HIGHEST = lax.Precision.HIGHEST
VMEM = pltpu.VMEM
SMEM = pltpu.SMEM
HBM = pltpu.HBM


def tables():
    outer = np.arange(OUTER)[:, None]
    inner = np.arange(INNER)[None, :]
    twist = 2.0 * math.pi * outer * inner / SAMPLES
    grid = 2.0 * math.pi * np.outer(np.arange(INNER), np.arange(INNER)) / INNER
    cos_in, sin_in = np.cos(grid), np.sin(grid)
    forward = np.block([[cos_in, -sin_in], [sin_in, cos_in]])
    inverse = np.block([[cos_in, sin_in], [-sin_in, cos_in]]) / SAMPLES
    index = outer + OUTER * inner
    signed = (index + SAMPLES // 2) % SAMPLES - SAMPLES // 2
    freq = signed / SAMPLES
    log_freq = np.where(signed == 0, -1e30, np.log(np.maximum(np.abs(freq), 1e-9)))
    lag = np.where(signed == -(SAMPLES // 2), 0.0, 2.0 * math.pi * freq)
    rows = np.concatenate([np.cos(twist), np.sin(twist), log_freq, lag], axis=0)
    rows, forward, inverse = [np.asarray(t, np.float32) for t in (rows, forward, inverse)]
    top = inverse.astype(jnp.bfloat16)
    rest = (inverse - top.astype(np.float32)).astype(jnp.bfloat16)
    return rows, forward, np.stack([top, rest])


def transform(points, sign):
    count = len(points)
    if count == 1:
        return points
    even = transform(points[0::2], sign)
    odd = transform(points[1::2], sign)
    first, second = [], []
    half = count // 2
    for k in range(half):
        re, im = odd[k]
        angle = sign * 2.0 * math.pi * k / count
        c, s = math.cos(angle), math.sin(angle)
        if k == 0:
            tr, ti = re, im
        elif 4 * k == count:
            tr, ti = (-im, re) if sign > 0 else (im, -re)
        else:
            tr, ti = c * re - s * im, c * im + s * re
        er, ei = even[k]
        first.append((er + tr, ei + ti))
        second.append((er - tr, ei - ti))
    return first + second


def split(x):
    top = x.astype(jnp.bfloat16)
    return top, (x - top.astype(jnp.float32)).astype(jnp.bfloat16)


def product(left, right, dims=(((1,), (0,)), ((), ()))):
    def dot(a, b):
        return lax.dot_general(a, b, dims, preferred_element_type=jnp.float32)

    return dot(left[0], right[0]) + (dot(left[0], right[1]) + dot(left[1], right[0]))


def column(row):
    rows = lax.broadcasted_iota(jnp.int32, (DETS, DETS), 0)
    cols = lax.broadcasted_iota(jnp.int32, (DETS, DETS), 1)
    return jnp.sum(jnp.where(rows == cols, row, 0.0), axis=1, keepdims=True)


def ranks(slots, counts, mark):
    for block in range(PEERS):
        counts[block] = 0
    for entry in range(PEERS):
        slot = slots[0, entry]
        block = slot >> 2
        rank = counts[block]
        counts[block] = rank + 1
        mark(entry, slot, block, rank)


def forward_kernel(
    slots_h, signal_h, tau_h, knee_h, slope_h, white_h, mix_h, rows_h, matrix_h,
    out, scratch, slots, signal, tau, knee, slope, white, mix, rows, matrix,
    counts, sems,
):
    pairs = [
        (signal_h.at[0], signal), (rows_h, rows), (slots_h, slots), (tau_h, tau),
        (knee_h, knee), (slope_h, slope), (white_h, white), (mix_h.at[0], mix),
        (matrix_h, matrix),
    ]
    copies = [pltpu.make_async_copy(a, b, sems.at[i]) for i, (a, b) in enumerate(pairs)]
    for copy in copies:
        copy.start()
    for copy in copies[2:8]:
        copy.wait()
    mixed = jnp.concatenate([mix[0:8, :], mix[8:16, :]], axis=1)
    for k in range(OUTER):
        out[k, 32:40, :] = mixed
        out[k, 40:48, :] = jnp.full((8, INNER), -1.0, jnp.float32)

    def mark(entry, slot, block, rank):
        value = (slot - 4 * block).astype(jnp.float32)
        out[block, pl.ds(40 + rank, 1), :] = jnp.broadcast_to(value, (1, INNER))

    ranks(slots, counts, mark)
    for copy in copies[0:2]:
        copy.wait()
    for half in range(2):
        lo = 8 * half
        points = [
            (
                signal[lo : lo + 8, a * INNER : (a + 1) * INNER],
                signal[lo : lo + 8, (OUTER + a) * INNER : (OUTER + a + 1) * INNER],
            )
            for a in range(OUTER)
        ]
        for k, (re, im) in enumerate(transform(points, -1)):
            c = rows[k : k + 1, :]
            s = rows[OUTER + k : OUTER + k + 1, :]
            scratch[k * DETS + lo : k * DETS + lo + 8, 0:INNER] = re * c + im * s
            scratch[k * DETS + lo : k * DETS + lo + 8, INNER : 2 * INNER] = im * c - re * s
    tau_c, knee_p, slope_c, white_c = noise_params(tau, knee, slope, white)
    copies[8].wait()
    group = 8
    for start in range(0, OUTER, group):
        spec = jnp.dot(
            scratch[start * DETS : (start + group) * DETS, :],
            matrix[...],
            precision=HIGHEST,
            preferred_element_type=jnp.float32,
        )
        for step in range(group):
            k = start + step
            power = jnp.exp(slope_c * rows[2 * OUTER + k : 2 * OUTER + k + 1, :])
            weight = white_c * power / (power + knee_p)
            lag = tau_c * rows[3 * OUTER + k : 3 * OUTER + k + 1, :]
            re = spec[step * DETS : (step + 1) * DETS, 0:INNER]
            im = spec[step * DETS : (step + 1) * DETS, INNER : 2 * INNER]
            out[k, 0:DETS, :] = weight * (re - lag * im)
            out[k, DETS : 2 * DETS, :] = weight * (im + lag * re)


def couple_kernel(got, coupling_h, out, labels, coupling, sem):
    copy = pltpu.make_async_copy(coupling_h, coupling, sem)
    copy.start()
    amps = None
    mixes = []
    for half in range(2):
        lo = 8 * half
        re = got[:, lo : lo + 8, :].reshape(PEERS * 8, INNER)
        im = got[:, DETS + lo : DETS + lo + 8, :].reshape(PEERS * 8, INNER)
        mix = split(
            got[:, 32:40, half * MODES : (half + 1) * MODES].reshape(PEERS * 8, MODES)
        )
        both = split(jnp.concatenate([re, im], axis=1))
        part = product(mix, both, (((0,), (0,)), ((), ())))
        amps = part if amps is None else amps + part
        mixes.append(mix)
    copy.wait()
    coupled = split(product(split(coupling[...]), split(amps)))
    for half in range(2):
        lo = 8 * half
        back = product(mixes[half], coupled)
        out[:, lo : lo + 8, :] = back[:, 0:INNER].reshape(PEERS, 8, INNER)
        out[:, DETS + lo : DETS + lo + 8, :] = back[:, INNER:].reshape(PEERS, 8, INNER)
    labels[...] = got[:, 40:48, :]


def lane_marks():
    lanes = lax.broadcasted_iota(jnp.int32, (INNER, INNER), 1).astype(jnp.float32)
    return (
        lanes.astype(jnp.bfloat16),
        jnp.ones((INNER, INNER), jnp.bfloat16),
        jnp.zeros((INNER, INNER), jnp.bfloat16),
    )


def noise_params(tau, knee, slope, white):
    def wide(ref):
        return jnp.broadcast_to(column(ref[...]), (DETS, INNER))

    slope_c = wide(slope)
    return wide(tau), jnp.exp(slope_c * jnp.log(wide(knee))), slope_c, wide(white)


def hot_kernel(pixel, knee, slope, white, log_f, hot, lows, weight):
    lanes, one, none = lane_marks()
    pieces = [pixel[0, :, i * INNER : (i + 1) * INNER] & 127 for i in range(UNROLL)]
    turned = jnp.concatenate(pieces, axis=0).astype(jnp.float32).T
    lows[0] = turned
    for step in range(UNROLL):
        for d in range(0, DETS, HOT):
            at = step * DETS + d
            low_d = jnp.broadcast_to(turned[:, at : at + 1], (INNER, INNER))
            hot[0, at // HOT] = jnp.where(low_d.astype(jnp.bfloat16) == lanes, one, none)
    _, knee_p, slope_c, white_c = noise_params(knee, knee, slope, white)
    for k in range(weight.shape[0]):
        power = jnp.exp(slope_c * log_f[0, k : k + 1, :])
        weight[k] = white_c * power / (power + knee_p)


def bin_kernel(
    slots_h, tiles_h, weighted, weight, back, cosine, sine, pixel_h, rows_h, matrix_h,
    lows_h, hot_h, out, scratch, stream, slots, tiles, pixel, rows, matrix, counts, parts,
    even, odd, hot, lows, sems, hot_sems, low_sems,
):
    pairs = [
        (matrix_h, matrix), (rows_h, rows), (slots_h, slots), (tiles_h.at[0], tiles),
        (pixel_h.at[0], pixel),
    ]
    copies = [pltpu.make_async_copy(a, b, sems.at[i]) for i, (a, b) in enumerate(pairs)]
    for copy in copies:
        copy.start()

    def load(start, slot):
        return (
            pltpu.make_async_copy(hot_h.at[start], hot.at[slot], hot_sems.at[slot]),
            pltpu.make_async_copy(lows_h.at[start], lows.at[slot], low_sems.at[slot]),
        )

    for copy in load(0, 0):
        copy.start()
    def clear(entry, carry):
        blank = jnp.zeros((ROWS, INNER), jnp.float32)
        even[entry] = blank
        odd[entry] = blank
        out[entry] = blank
        out[PEERS + entry] = blank
        return carry

    lax.fori_loop(0, PEERS, clear, 0)
    for k in range(OUTER):
        re = weighted[k, 0:DETS, :] - weight[k] * back[k, 0:DETS, :]
        im = weighted[k, DETS : 2 * DETS, :] - weight[k] * back[k, DETS : 2 * DETS, :]
        scratch[k * DETS : (k + 1) * DETS, 0:INNER] = re
        scratch[k * DETS : (k + 1) * DETS, INNER : 2 * INNER] = im
    for copy in copies[0:2]:
        copy.wait()
    group = 8
    for start in range(0, OUTER, group):
        section = product(
            split(scratch[start * DETS : (start + group) * DETS, :]), (matrix[0], matrix[1])
        )
        for step in range(group):
            k = start + step
            c = rows[k : k + 1, :]
            s = rows[OUTER + k : OUTER + k + 1, :]
            re = section[step * DETS : (step + 1) * DETS, 0:INNER]
            im = section[step * DETS : (step + 1) * DETS, INNER : 2 * INNER]
            scratch[k * DETS : (k + 1) * DETS, 0:INNER] = re * c - im * s
            scratch[k * DETS : (k + 1) * DETS, INNER : 2 * INNER] = im * c + re * s
    for half in range(2):
        lo = 8 * half
        points = [
            (
                scratch[k * DETS + lo : k * DETS + lo + 8, 0:INNER],
                scratch[k * DETS + lo : k * DETS + lo + 8, INNER : 2 * INNER],
            )
            for k in range(OUTER)
        ]
        for a, (re, im) in enumerate(transform(points, 1)):
            stream[a, lo : lo + 8, :] = re
            stream[OUTER + a, lo : lo + 8, :] = im

    for copy in copies[2:]:
        copy.wait()
    levels = (lax.broadcasted_iota(jnp.int32, (16, INNER), 0) & 7).astype(jnp.float32)
    marks = [(levels + 8.0 * g).astype(jnp.bfloat16) for g in range(2)]
    zero = jnp.zeros((16, INNER), jnp.bfloat16)
    lanes, one, none = lane_marks()

    def block(start, carry):
        slot = start & 1
        for copy in load(start, slot):
            copy.wait()

        @pl.when(start + 1 < STRIPS // UNROLL)
        def _():
            for copy in load(start + 1, 1 - slot):
                copy.start()

        for step in range(UNROLL):
            s = start * UNROLL + step
            base = pl.multiple_of(s * INNER, INNER)
            pix = pixel[:, pl.ds(base, INNER)]
            values = stream[s]
            maps = [
                values,
                values * cosine[:, pl.ds(base, INNER)],
                values * sine[:, pl.ds(base, INNER)],
            ]
            tops = [m.astype(jnp.bfloat16).astype(jnp.float32) for m in maps]
            rests = [m - t for m, t in zip(maps, tops)]
            for i, field in enumerate([(pix >> 7).astype(jnp.float32)] + tops + rests):
                at = (step * 7 + i) * DETS
                parts[at : at + DETS, :] = field
        for step in range(UNROLL):
            s = start * UNROLL + step

            def spread(i, j, d):
                lines = [
                    parts[pl.ds((step * 7 + n) * DETS + d, 8, stride=0), :] for n in (i, j)
                ]
                return jnp.concatenate(lines, axis=0).astype(jnp.bfloat16)

            for d in range(DETS):
                at = step * DETS + d
                high_d = spread(0, 0, d)
                hits = [high_d == mark for mark in marks]
                left = []
                for c in range(3):
                    both = spread(1 + c, 4 + c, d)
                    left += [jnp.where(hit, both, zero) for hit in hits]
                left = jnp.concatenate(left, axis=0)
                if d % HOT == 0:
                    right = hot[slot, at // HOT]
                else:
                    low_d = jnp.broadcast_to(lows[slot, :, at : at + 1], (INNER, INNER))
                    right = jnp.where(low_d.astype(jnp.bfloat16) == lanes, one, none)
                sums = jnp.dot(left, right, preferred_element_type=jnp.float32)
                tile = tiles[d, s]
                total = (even, odd)[d % 2]
                sums = sums.reshape(6, 2, 8, INNER)
                total[tile] = total[tile] + (sums[:, 0] + sums[:, 1]).reshape(ROWS, INNER)
        return carry

    lax.fori_loop(0, STRIPS // UNROLL, block, 0)

    def settle(entry, slot, home, rank):
        out[2 * home + rank] = even[entry] + odd[entry]

    ranks(slots, counts, settle)


def gather_kernel(homes, got, labels, out):
    for place in range(2 * TM):
        out[place, 0:ROWS, :] = jnp.zeros((ROWS, INNER), jnp.float32)
        out[place, ROWS:, :] = jnp.full((8, INNER), -1.0, jnp.float32)
    def add(source, totals):
        totals = list(totals)
        for rank in range(2):
            slab = got[source, rank * ROWS : (rank + 1) * ROWS, :]
            label = labels[source, rank : rank + 1, :]
            for tile in range(4):
                totals[tile] = totals[tile] + jnp.where(label == float(tile), slab, 0.0)
        return tuple(totals)

    blank = jnp.zeros((ROWS, INNER), jnp.float32)
    totals = lax.fori_loop(0, PEERS, add, (blank,) * 4, unroll=4)
    for tile in range(4):
        total = totals[tile]
        owner = homes[0, tile] // OWN
        rank = 0
        for other in range(tile):
            rank = rank + jnp.where(homes[0, other] // OWN == owner, 1, 0)
        row = 2 * owner + rank
        out[row, 0:ROWS, :] = total
        place = (homes[0, tile] - OWN * owner).astype(jnp.float32)
        out[row, ROWS:, :] = jnp.broadcast_to(place, (8, INNER))


def place_kernel(got, out, totals):
    for place in range(OWN):
        total = jnp.zeros((ROWS, INNER), jnp.float32)
        for source in range(2 * TM):
            hit = got[source, ROWS : ROWS + 1, :] == float(place)
            total = total + jnp.where(hit, got[source, 0:ROWS, :], 0.0)
        totals[place * ROWS : (place + 1) * ROWS, :] = total
    for row in range(ROWS):
        at = (row % 16) * INNER
        out[row // 16, :, at : at + INNER] = totals[pl.ds(row, OWN, stride=ROWS), :]


def call(kernel, outs, specs, *operands, scratch=()):
    operands = [
        pltpu.with_memory_space_constraint(o, HBM) if m is HBM else o
        for o, m in zip(operands, specs)
    ]
    return pl.pallas_call(
        kernel,
        out_shape=outs,
        in_specs=[pl.BlockSpec(memory_space=s) for s in specs],
        scratch_shapes=list(scratch),
        compiler_params=pltpu.CompilerParams(vmem_limit_bytes=9 << 20),
    )(*operands)


def per_device(
    timestream, polar_angle, pixel_index, strip_tile, time_const, knee_freq, noise_slope,
    white_weight, mode_mix, coupling, device_slots, slot_home,
):
    f32 = jnp.float32
    table, forward, inverse = tables()
    rows, forward, inverse = [jnp.asarray(t) for t in (table, forward, inverse)]
    packed = call(
        forward_kernel,
        jax.ShapeDtypeStruct((PEERS, 48, INNER), f32),
        [HBM] * 9,
        device_slots, timestream, time_const, knee_freq, noise_slope, white_weight,
        mode_mix, rows, forward,
        scratch=[
            VMEM((OUTER * DETS, 2 * INNER), f32),
            SMEM((1, PEERS), jnp.int32),
            VMEM((DETS, 2 * SAMPLES), f32),
            VMEM((1, DETS), f32),
            VMEM((1, DETS), f32),
            VMEM((1, DETS), f32),
            VMEM((1, DETS), f32),
            VMEM((DETS, MODES), f32),
            VMEM((4 * OUTER, INNER), f32),
            VMEM((2 * INNER, 2 * INNER), f32),
            SMEM((PEERS,), jnp.int32),
            pltpu.SemaphoreType.DMA((9,)),
        ],
    )
    got = lax.all_to_all(packed, "det", 0, 0, tiled=True)
    projected, labels = call(
        couple_kernel,
        (
            jax.ShapeDtypeStruct((PEERS, 2 * DETS, INNER), f32),
            jax.ShapeDtypeStruct((PEERS, 8, INNER), f32),
        ),
        [VMEM, HBM],
        got, coupling,
        scratch=[VMEM((MODES, MODES), f32), pltpu.SemaphoreType.DMA],
    )
    back = lax.all_to_all(projected, "det", 0, 0, tiled=True)
    blocks = STRIPS // UNROLL
    width = UNROLL * INNER
    halves = UNROLL * DETS // HOT
    ks = OUTER // blocks
    hot, lows, weight = pl.pallas_call(
        hot_kernel,
        out_shape=(
            HBM((blocks, halves, INNER, INNER), jnp.bfloat16),
            HBM((blocks, INNER, UNROLL * DETS), f32),
            jax.ShapeDtypeStruct((OUTER, DETS, INNER), f32),
        ),
        grid=(blocks,),
        in_specs=[pl.BlockSpec((1, DETS, width), lambda i: (0, 0, i))]
        + [pl.BlockSpec((1, DETS), lambda i: (0, 0))] * 3
        + [pl.BlockSpec((1, ks, INNER), lambda i: (i, 0, 0))],
        out_specs=(
            pl.BlockSpec((1, halves, INNER, INNER), lambda i: (i, 0, 0, 0)),
            pl.BlockSpec((1, INNER, UNROLL * DETS), lambda i: (i, 0, 0)),
            pl.BlockSpec((ks, DETS, INNER), lambda i: (i, 0, 0)),
        ),
        compiler_params=pltpu.CompilerParams(vmem_limit_bytes=9 << 20),
    )(
        pltpu.with_memory_space_constraint(pixel_index, HBM), knee_freq, noise_slope, white_weight,
        jnp.asarray(table[2 * OUTER : 3 * OUTER].reshape(blocks, ks, INNER)),
    )
    twice = 2.0 * polar_angle[0]
    partials = call(
        bin_kernel,
        jax.ShapeDtypeStruct((2 * PEERS, ROWS, INNER), f32),
        [HBM] * 2 + [VMEM] * 5 + [HBM] * 5,
        device_slots, strip_tile, packed, weight, back, jnp.cos(twice), jnp.sin(twice),
        pixel_index, rows, inverse, lows, hot,
        scratch=[
            VMEM((OUTER * DETS, 2 * INNER), f32),
            VMEM((STRIPS, DETS, INNER), f32),
            SMEM((1, PEERS), jnp.int32),
            SMEM((DETS, STRIPS), jnp.int32),
            VMEM((DETS, 2 * SAMPLES), jnp.int32),
            VMEM((4 * OUTER, INNER), f32),
            VMEM((2, 2 * INNER, 2 * INNER), jnp.bfloat16),
            SMEM((PEERS,), jnp.int32),
            VMEM((UNROLL * 7 * DETS, INNER), f32),
            VMEM((PEERS, ROWS, INNER), f32),
            VMEM((PEERS, ROWS, INNER), f32),
            VMEM((2, UNROLL * DETS // HOT, INNER, INNER), jnp.bfloat16),
            VMEM((2, INNER, UNROLL * DETS), f32),
            pltpu.SemaphoreType.DMA((5,)),
            pltpu.SemaphoreType.DMA((2,)),
            pltpu.SemaphoreType.DMA((2,)),
        ],
    )
    parts = lax.all_to_all(
        partials.reshape(PEERS, 2 * ROWS, INNER), "det", 0, 0, tiled=True
    )
    owned = call(
        gather_kernel,
        jax.ShapeDtypeStruct((2 * TM, ROWS + 8, INNER), f32),
        [SMEM] + [VMEM] * 2,
        slot_home, parts, labels,
    )
    final = lax.all_to_all(
        owned.reshape(TM, 2 * (ROWS + 8), INNER), "tm", 0, 0, tiled=True
    )
    placed = call(
        place_kernel,
        jax.ShapeDtypeStruct((3, OWN, 16 * INNER), f32),
        [VMEM],
        final.reshape(2 * TM, ROWS + 8, INNER),
        scratch=[VMEM((OWN * ROWS, INNER), f32)],
    )
    return placed.transpose(1, 0, 2)


def solution(mesh):
    strips = P("tm", "det", None)
    dets = P("tm", "det")
    return jax.shard_map(
        per_device,
        mesh=mesh,
        in_specs=(strips,) * 4 + (dets,) * 4 + (strips, P(), dets, dets),
        out_specs=P(("tm", "det"), None, None),
        check_vma=False,
    )
```
